512 devices in a mesh: expert: 128 (over z, y, core), etp: 4 (over x).
Axes of the slice: x: 4, y: 8, z: 8, core: 2. Of those that a mesh axis runs over, the one named last changes fastest.
Arguments:
- tokens: bfloat16 [16384, 2048], P('expert', 'etp'), may hold values from -6 to 6
- out_grad: bfloat16 [16384, 2048], P('expert', 'etp'), may hold values from -12 to 12
- routes: int32 [16384, 8], P('expert'), may hold values from 0 to 127, all different within a row; in each aligned block of 128 rows (0 to 127, 128 to 255, ...) at most 9 rows name the same one
- combine: float32 [16384, 8], P('expert'), may hold values from 0.02 to 0.5
- w_gate: bfloat16 [128, 768, 2048], P('expert', 'etp'), may hold values from -0.125 to 0.125
- w_up: bfloat16 [128, 768, 2048], P('expert', 'etp'), may hold values from -0.125 to 0.125
- w_down: bfloat16 [128, 768, 2048], P('expert', 'etp'), may hold values from -0.21875 to 0.21875
Outputs:
- grad_tokens: bfloat16 [16384, 2048], P('expert', 'etp')
- grad_gate: bfloat16 [128, 768, 2048], P('expert', 'etp')
- grad_up: bfloat16 [128, 768, 2048], P('expert', 'etp')
- grad_down: bfloat16 [128, 768, 2048], P('expert', 'etp')
The draws below stay inside these ranges and needn't reach their ends.
Inputs may be any that keep to these rules, and one draw needn't show every extreme that they name: `routes`: each row names 8 different experts. Within each aligned block of 128 rows (the rows of one index of expert) no expert is named by more than 9 rows, and in some block one expert is named by exactly 9 rows.
All inputs are finite; a program needn't handle non-finite values.
Results may differ from the reference program's by a relative error of at most 0.0064.
Values may be sent and summed in bfloat16 or wider, within the bound.
A program may use at most 128 MiB of HBM per device.

```python
import math
import jax
import jax.numpy as jnp
import numpy as np
from jax import lax

D = 2048
H = 768
TOP = 8
TOK_DEV = 128
EXPERTS = 128
CAP = 9
TOKENS = 16384
N_EXPERT = 128


def level_of(rng, dims, cuts, smallest, largest):
    def one(dim, parts):
        draws = jax.random.uniform(jax.random.fold_in(jax.random.fold_in(rng, 6), dim), (parts,), jnp.float32, smallest / len(cuts), largest / len(cuts))
        return jnp.repeat(jnp.exp(draws), dims[dim] // parts).reshape((-1,) + (1,) * (len(dims) - dim - 1))

    loudness = one(*cuts[0])
    for cut in cuts[1:]:
        loudness = loudness * one(*cut)
    return loudness


def assign_block(stream_key, own, number, rows, amount, top, bound, lean):
    ranking = jax.random.permutation(stream_key, amount)
    heavy_load, ordinary = shares(amount, rows * top, bound, lean, True), shares(amount, rows * top, bound, lean, False)
    places = jnp.arange(amount)

    def named(tallies, rotation):
        used = int((tallies > 0).sum())
        fixed = max(1, used // 4)
        passed = fixed + (places - fixed + rotation * (used - fixed)) % max(1, amount - fixed)
        return jnp.zeros((amount,), jnp.int32).at[ranking[jnp.where(places < fixed, places, passed)]].set(jnp.asarray(tallies, jnp.int32))

    tallies = jnp.where(number % 4 == 0, named(heavy_load, number // 4), named(ordinary, number - number // 4 - 1))
    mixed = jax.random.permutation(jax.random.fold_in(own, 3), amount)
    donor, receiver = mixed[0:amount // 2 * 2:2], mixed[1:amount // 2 * 2:2]
    slack = jnp.minimum(tallies[donor] - 1, bound - tallies[receiver]) // 2
    slack = jnp.where((donor == ranking[0]) | (receiver == ranking[0]) | (tallies[receiver] == 0), 0, jnp.maximum(slack, 0))
    passed = jax.random.randint(jax.random.fold_in(own, 4), (amount // 2,), 0, 1 << 20) % (slack + 1)
    tallies = tallies.at[donor].add(-passed).at[receiver].add(passed)
    members = jnp.searchsorted(jnp.cumsum(tallies), jnp.arange(rows * top), side="right").astype(jnp.int32)
    table = members.reshape(top, rows).T
    table = table[jax.random.permutation(jax.random.fold_in(own, 1), rows)]
    rotation = jax.random.randint(jax.random.fold_in(own, 2), (rows, 1), 0, top)
    return jnp.take_along_axis(table, (jnp.arange(top)[None, :] + rotation) % top, axis=1)


def shares(count, total, bound, lean, full):
    loads = [(1 << 20) // math.isqrt(standing ** lean) + 1 for standing in range(1, count + 1)]
    largest = bound if full else min(bound, max(-(-total // count), total * loads[0] // sum(loads)))
    least = 1 if total - largest >= count - 1 else 0
    holding, surplus = [largest] + [least] * (count - 1), total - largest - least * (count - 1)
    while surplus > 0:
        candidates = [i for i in range(1, count) if holding[i] < largest] or [i for i in range(1, count) if holding[i] < bound]
        whole, left = sum([loads[i] for i in candidates]), surplus
        for i in candidates:
            addition = min(bound - holding[i], max(1, left * loads[i] // whole), surplus)
            holding[i] = holding[i] + addition
            surplus = surplus - addition
    return np.array(holding)


def gaussian(key, dims, deviation, limit, pieces=(), held_as=jnp.bfloat16):
    drawn = jax.random.normal(key, dims, jnp.float32) * deviation
    if len(pieces) > 0:
        drawn = level_of(key, dims, pieces, -0.22, 0.18) * drawn
    return jnp.clip(drawn, min=-limit, max=limit).astype(held_as)


def setup_inputs(seed: int = 0) -> dict:
    arg_keys = jax.random.split(jax.random.key(seed), 8)
    tokens = gaussian(arg_keys[0], (TOKENS, D), 1.0, 6.0, ((0, 128), (1, 4)))
    out_grad = gaussian(arg_keys[1], (TOKENS, D), 2.0, 12.0, ((0, 128), (1, 4)))
    routes_keys = jax.random.split(jax.random.fold_in(arg_keys[2], 1), TOKENS // TOK_DEV)
    routes_turns = jax.random.permutation(jax.random.fold_in(arg_keys[2], 3), TOKENS // TOK_DEV)
    routes = jax.vmap(lambda own, number: assign_block(jax.random.fold_in(arg_keys[2], 2), own, number, TOK_DEV, EXPERTS, TOP, CAP, 1))(routes_keys, routes_turns).reshape((TOKENS, TOP))
    combine = jnp.clip(jnp.exp(math.log(0.5) - 3.218876 * jax.random.uniform(arg_keys[3], (TOKENS, TOP), jnp.float32) ** level_of(arg_keys[3], (TOKENS, TOP), ((0, 128),), -0.2, 0.2)), 0.02, 0.5)
    w_gate = gaussian(arg_keys[4], (EXPERTS, H, D), D ** -0.5, 0.125, ((0, 128), (1, 4)))
    w_up = gaussian(arg_keys[5], (EXPERTS, H, D), D ** -0.5, 0.125, ((0, 128), (1, 4)))
    w_down = gaussian(arg_keys[6], (EXPERTS, H, D), H ** -0.5, 0.21875, ((0, 128), (1, 4)))
    return dict(tokens=tokens, out_grad=out_grad, routes=routes, combine=combine, w_gate=w_gate, w_up=w_up, w_down=w_down)


def routing_table(routes):
    blocks = routes.reshape(N_EXPERT, TOK_DEV * TOP)
    labels = jnp.arange(EXPERTS, dtype=jnp.int32)

    def place(block_routes):
        one_hot = (block_routes[:, None] == labels[None, :]).astype(jnp.int32)
        earlier = jnp.cumsum(one_hot, axis=0) - one_hot
        return jnp.sum(earlier * one_hot, axis=1).astype(jnp.int32)

    position = jax.vmap(place)(blocks)
    anchor = jnp.arange(N_EXPERT, dtype=jnp.int32)[:, None]
    slot = blocks * (N_EXPERT * CAP) + anchor * CAP + position
    filler = TOKENS * TOP
    table = jnp.full((EXPERTS * N_EXPERT * CAP,), filler, jnp.int32)
    table = table.at[slot.reshape(-1)].set(jnp.arange(filler, dtype=jnp.int32))
    return table.reshape(EXPERTS, N_EXPERT * CAP)


def reference(tokens, out_grad, routes, combine, w_gate, w_up, w_down):
    table = routing_table(routes)
    filler = TOKENS * TOP
    weights_flat = combine.reshape(-1)

    def expert_step(grad_total, operands):
        rows, gate_w, up_w, down_w = operands
        is_live = rows < filler
        safe_rows = jnp.minimum(rows, filler - 1)
        token_of = safe_rows // TOP
        rows_x = tokens[token_of] * is_live[:, None].astype(tokens.dtype)
        scale = weights_flat[safe_rows] * is_live.astype(weights_flat.dtype)
        rows_g = (scale[:, None] * out_grad[token_of].astype(jnp.float32)).astype(jnp.bfloat16)
        gate = jnp.dot(rows_x, gate_w.T, preferred_element_type=jnp.float32)
        up = jnp.dot(rows_x, up_w.T, preferred_element_type=jnp.float32)
        hidden_grad = jnp.dot(rows_g, down_w.T, preferred_element_type=jnp.float32)
        sigma = jax.nn.sigmoid(gate)
        silu = gate * sigma
        acts = (silu * up).astype(jnp.bfloat16)
        grad_down = jnp.dot(acts.T, rows_g, preferred_element_type=jnp.float32).astype(jnp.bfloat16)
        gate_term = (hidden_grad * up * sigma * (1.0 + gate * (1.0 - sigma))).astype(jnp.bfloat16)
        up_term = (hidden_grad * silu).astype(jnp.bfloat16)
        grad_gate = jnp.dot(gate_term.T, rows_x, preferred_element_type=jnp.float32).astype(jnp.bfloat16)
        grad_up = jnp.dot(up_term.T, rows_x, preferred_element_type=jnp.float32).astype(jnp.bfloat16)
        slot_grads = (jnp.dot(gate_term, gate_w, preferred_element_type=jnp.float32)
                      + jnp.dot(up_term, up_w, preferred_element_type=jnp.float32)).astype(jnp.bfloat16)
        target = jnp.where(is_live, token_of, TOKENS)
        grad_total = grad_total.at[target].add(slot_grads.astype(jnp.float32), mode="drop")
        return grad_total, (grad_gate, grad_up, grad_down)

    start_total = jnp.zeros((TOKENS, D), jnp.float32)
    grad_total, (grad_gate, grad_up, grad_down) = lax.scan(expert_step, start_total, (table, w_gate, w_up, w_down))
    return grad_total.astype(jnp.bfloat16), grad_gate, grad_up, grad_down
```

```python
import functools

import jax
import jax.numpy as jnp
from jax import lax
from jax.experimental import pallas as pl
from jax.experimental.pallas import tpu as pltpu
from jax.sharding import PartitionSpec as P

MESH = pl.DeviceIdType.MESH
BF16 = jnp.bfloat16
F32 = jnp.float32
LANES = 128
MAIN = 8
STRIDE = 37
CHUNKS = 8


def dot(a, b, dims=(((1,), (0,)), ((), ()))):
    return lax.dot_general(a, b, dims, preferred_element_type=F32)


LAST = (((1,), (1,)), ((), ()))
FIRST = (((0,), (0,)), ((), ()))


def kernel(
    n_e, n_x, nq,
    tokens, grads, routes, combine, wg_h, wu_h, wd_h,
    o_tok, o_gate, o_up, o_down,
    wg, wu, wd, wsw, place_t, weight_t, pt, pot, ovf, send, gath, ovs, xs, gs,
    acts, terms, back, ret,
    w_sem, ws_s, ws_r, a_s, a_r, g1_s, g1_r, g2_s, g2_r, t1_s, t1_r, t2_s, t2_r, b_s, b_r,
):
    tok, feat = tokens.shape
    top = routes.shape[1]
    nc = feat // LANES
    hid = wg.shape[0]
    ns = n_e // nq
    rows = ns * (MAIN + 1)
    half = ns // 2
    cut = (rows // 2 + 15) // 16 * 16
    me = lax.axis_index("expert")
    xi = lax.axis_index("etp")
    right = lax.rem(xi + 1, n_x)
    left = lax.rem(xi + n_x - 1, n_x)

    def remote(src, dst, s, r, dev):
        return pltpu.make_async_remote_copy(
            src_ref=src, dst_ref=dst, send_sem=s, recv_sem=r, device_id=dev, device_id_type=MESH
        )

    def drain(ref, sem):
        pltpu.make_async_copy(ref, ref, sem).wait()

    bar = pltpu.get_barrier_semaphore()

    def greet(off, carry):
        pl.semaphore_signal(
            bar, inc=1, device_id={"expert": lax.rem(me + off, n_e)}, device_id_type=MESH
        )
        return carry

    lax.fori_loop(1, n_e, greet, 0)
    for d in range(1, n_x):
        pl.semaphore_signal(
            bar, inc=1, device_id={"etp": lax.rem(xi + d, n_x)}, device_id_type=MESH
        )

    loads = [
        pltpu.make_async_copy(src, dst, w_sem.at[n])
        for n, (src, dst) in enumerate(((wg_h, wg), (wu_h, wu), (wd_h, wd)))
    ]
    for load in loads:
        load.start()

    chosen = routes[...]
    share = combine[...]
    label = lax.broadcasted_iota(jnp.int32, (tok, n_e), 1)
    hit = jnp.zeros((tok, n_e), F32)
    weight = jnp.zeros((tok, n_e), F32)
    for k in range(top):
        same = chosen[:, k : k + 1] == label
        hit = hit + jnp.where(same, 1.0, 0.0)
        weight = weight + jnp.where(same, share[:, k : k + 1], 0.0)
    lower = (
        lax.broadcasted_iota(jnp.int32, (tok, tok), 0)
        > lax.broadcasted_iota(jnp.int32, (tok, tok), 1)
    )
    lower = jnp.where(lower, 1.0, 0.0).astype(BF16)
    place = jnp.where(hit > 0.5, dot(lower, hit.astype(BF16)), -1.0)
    place_t[...] = place.T
    weight_t[...] = weight.T

    slot_id = lax.broadcasted_iota(jnp.int32, (MAIN, tok), 0).astype(F32)

    def pack(b, carry):
        base = b * ns
        hits, scales = [], []
        for u in range(ns):
            row = jnp.broadcast_to(place_t[pl.ds(base + u, 1), :], (MAIN, tok))
            wrow = jnp.broadcast_to(weight_t[pl.ds(base + u, 1), :], (MAIN, tok))
            same = row == slot_id
            hits.append(jnp.where(same, 1.0, 0.0))
            scales.append(jnp.sum(jnp.where(same, wrow, 0.0), axis=1, keepdims=True))
        pick = jnp.concatenate(hits, axis=0)
        scale = jnp.concatenate(scales, axis=0)
        pt[b] = pick.T.astype(BF16)
        pick = pick.astype(BF16)
        x = dot(pick, tokens[...])
        g = dot(pick, grads[...]) * scale
        for c in range(nc):
            cols = slice(c * LANES, (c + 1) * LANES)
            send[pl.ds(base, ns), c] = x[:, cols].reshape(ns, MAIN, LANES).astype(BF16)
            send[pl.ds(base, ns), nc + c] = g[:, cols].reshape(ns, MAIN, LANES).astype(BF16)
        return carry

    lax.fori_loop(0, nq, pack, 0)
    same = place_t[...] == float(MAIN)
    scale = jnp.sum(jnp.where(same, weight_t[...], 0.0), axis=1, keepdims=True)
    pick = jnp.where(same, 1.0, 0.0)
    pot[...] = pick.T.astype(BF16)
    pick = pick.astype(BF16)
    x = dot(pick, tokens[...])
    g = dot(pick, grads[...]) * scale
    for c in range(nc):
        cols = slice(c * LANES, (c + 1) * LANES)
        ovf[:, c, :] = x[:, cols]
        ovf[:, nc + c, :] = g[:, cols]
    send[:, 2 * nc] = ovf[...].astype(BF16)

    pl.semaphore_wait(bar, n_e - 1 + n_x - 1)

    def swap(n, src, d):
        j = lax.rem(xi + d, n_x)
        cols = pl.ds(pl.multiple_of(j * feat, LANES), feat)
        return remote(
            src.at[:, cols], wsw.at[xi, pl.ds(n * hid, hid)],
            ws_s.at[n, d], ws_r.at[n, d], {"etp": j},
        )

    own_cols = pl.ds(pl.multiple_of(xi * feat, LANES), feat)
    own_swap = [
        pltpu.make_async_copy(src.at[:, own_cols], wsw.at[xi, pl.ds(n * hid, hid)], ws_r.at[n, 0])
        for n, src in enumerate((wg_h, wu_h))
    ]
    for n, src in enumerate((wg_h, wu_h)):
        own_swap[n].start()
        for d in range(1, n_x):
            swap(n, src, d).start()

    own = pltpu.make_async_copy(send.at[me], gath.at[xi, 0], a_r.at[0])
    own.start()

    def dispatch(k, carry):
        dest = lax.rem(me + lax.rem(k * STRIDE, n_e), n_e)
        q = k // ns
        remote(send.at[dest], gath.at[xi, k], a_s.at[q], a_r.at[q], {"expert": dest}).start()
        return carry

    lax.fori_loop(1, n_e, dispatch, 0)

    for load in loads:
        load.wait()

    def to_right(ref, s, r, n, q):
        return remote(ref, ref, s.at[n, q], r.at[n, q], {"etp": right})

    def to_left(ref, s, r, n, q):
        return remote(ref, ref, s.at[n, q], r.at[n, q], {"etp": left})

    def stage1(q):
        mine = gath.at[xi, pl.ds(q * ns, ns)]
        drain(mine, a_r.at[q])
        to_right(mine, g1_s, g1_r, 0, q).start()
        to_left(mine, g1_s, g1_r, 1, q).start()

    def stage2(q):
        drain(gath.at[left, pl.ds(q * ns, ns)], g1_r.at[0, q])
        to_right(gath.at[left, pl.ds(q * ns, half)], g2_s, g2_r, 0, q).start()
        drain(gath.at[right, pl.ds(q * ns, ns)], g1_r.at[1, q])
        to_left(gath.at[right, pl.ds(q * ns + half, ns - half)], g2_s, g2_r, 1, q).start()

    def stage3(q):
        far = lax.rem(xi + 2, n_x)
        base = q * ns
        drain(gath.at[far, pl.ds(base, half)], g2_r.at[0, q])
        drain(gath.at[far, pl.ds(base + half, ns - half)], g2_r.at[1, q])
        at = pl.multiple_of(q * rows, 16)
        over = pl.multiple_of(q * rows + ns * MAIN, 16)
        for j in range(n_x):
            ovs[...] = gath[j, pl.ds(base, ns), 2 * nc].astype(F32)
            for c in range(nc):
                cols = slice(j * feat + c * LANES, j * feat + (c + 1) * LANES)
                x = gath[j, pl.ds(base, ns), c]
                g = gath[j, pl.ds(base, ns), nc + c]
                xs[pl.ds(at, ns * MAIN), cols] = x.reshape(ns * MAIN, LANES)
                gs[pl.ds(at, ns * MAIN), cols] = g.reshape(ns * MAIN, LANES)
                xs[pl.ds(over, ns), cols] = ovs[:, c, :].astype(BF16)
                gs[pl.ds(over, ns), cols] = ovs[:, nc + c, :].astype(BF16)
        x = xs[pl.ds(at, rows), :]
        gate = dot(x, wg[...], LAST)
        up = dot(x, wu[...], LAST)
        hidden = dot(gs[pl.ds(at, rows), :], wd[...], LAST)
        sigma = jax.nn.sigmoid(gate)
        silu = gate * sigma
        acts[pl.ds(at, rows), :] = (silu * up).astype(BF16)
        gate_term = hidden * up * sigma * (1.0 + gate * (1.0 - sigma))
        up_term = hidden * silu
        both = jnp.concatenate([gate_term, up_term], axis=1)
        terms[xi, pl.ds(at, rows), :] = both.astype(BF16)
        mine = terms.at[xi, pl.ds(at, rows)]
        to_right(mine, t1_s, t1_r, 0, q).start()
        to_left(mine, t1_s, t1_r, 1, q).start()

    def stage4(q):
        at = pl.multiple_of(q * rows, 16)
        later = pl.multiple_of(q * rows + cut, 16)
        drain(terms.at[left, pl.ds(at, rows)], t1_r.at[0, q])
        to_right(terms.at[left, pl.ds(at, cut)], t2_s, t2_r, 0, q).start()
        drain(terms.at[right, pl.ds(at, rows)], t1_r.at[1, q])
        to_left(terms.at[right, pl.ds(later, rows - cut)], t2_s, t2_r, 1, q).start()

    def stage5(q):
        far = lax.rem(xi + 2, n_x)
        base = q * ns
        at = pl.multiple_of(q * rows, 16)
        later = pl.multiple_of(q * rows + cut, 16)
        drain(terms.at[far, pl.ds(at, cut)], t2_r.at[0, q])
        drain(terms.at[far, pl.ds(later, rows - cut)], t2_r.at[1, q])
        slot = dot(terms[0, pl.ds(at, rows), :], wsw[0])
        for j in range(1, n_x):
            slot = slot + dot(terms[j, pl.ds(at, rows), :], wsw[j])
        ovs[...] = jnp.zeros_like(ovs)
        for c in range(nc):
            cols = slice(c * LANES, (c + 1) * LANES)
            main = slot[: ns * MAIN, cols].reshape(ns, MAIN, LANES)
            back[pl.ds(base, ns), c] = main.astype(BF16)
            ovs[:, c, :] = slot[ns * MAIN :, cols]
        back[pl.ds(base, ns), nc] = ovs[...].astype(BF16)

        @pl.when(q == 0)
        def _():
            pltpu.make_async_copy(back.at[0], ret.at[me], b_r).start()

        def answer(k, carry):
            dest = lax.rem(me + n_e - lax.rem(k * STRIDE, n_e), n_e)
            remote(back.at[k], ret.at[me], b_s, b_r, {"expert": dest}).start()
            return carry

        lax.fori_loop(jnp.maximum(base, 1), base + ns, answer, 0)

    def step(t, carry):
        for lag, stage in enumerate((stage1, stage2, stage3, stage4, stage5)):
            q = t - lag
            if stage is stage5:

                @pl.when(q == 0)
                def _():
                    for n, src in enumerate((wg_h, wu_h)):
                        own_swap[n].wait()
                        for d in range(1, n_x):
                            swap(n, src, d).wait_recv()

            @pl.when(jnp.logical_and(q >= 0, q < nq))
            def _():
                stage(q)

        return carry

    lax.fori_loop(0, nq + 4, step, 0)

    mine = terms[xi]
    width = 2 * LANES
    for n in range(feat * n_x // width):
        cols = slice(n * width, (n + 1) * width)
        both = dot(mine, xs[:, cols], FIRST)
        o_gate[:, cols] = both[:hid].astype(BF16)
        o_up[:, cols] = both[hid:].astype(BF16)
        o_down[:, cols] = dot(acts[...], gs[:, cols], FIRST).astype(BF16)

    drain(ret, b_r)
    ovf[...] = ret[:, nc].astype(F32)
    for c in range(nc):
        total = dot(pot[...], ovf[:, c, :].astype(BF16))
        for b in range(nq):
            part = ret[pl.ds(b * ns, ns), c].reshape(ns * MAIN, LANES)
            total = total + dot(pt[b], part)
        o_tok[:, c * LANES : (c + 1) * LANES] = total.astype(BF16)

    for n, src in enumerate((wg_h, wu_h)):
        for d in range(1, n_x):
            swap(n, src, d).wait_send()
    drain(back.at[pl.ds(1, n_e - 1)], b_s)

    def flush(q, carry):
        at = pl.multiple_of(q * rows, 16)
        for n in range(2):
            drain(gath.at[0, pl.ds(q * ns, ns)], g1_s.at[n, q])
            drain(gath.at[0, pl.ds(q * ns, half)], g2_s.at[n, q])
            drain(terms.at[0, pl.ds(at, rows)], t1_s.at[n, q])
            drain(terms.at[0, pl.ds(at, cut if n == 0 else rows - cut)], t2_s.at[n, q])
        return carry

    lax.fori_loop(0, nq, flush, 0)
    drain(send.at[pl.ds(0, ns - 1)], a_s.at[0])

    def flush_a(q, carry):
        drain(send.at[pl.ds(0, ns)], a_s.at[q])
        return carry

    lax.fori_loop(1, nq, flush_a, 0)


def body(tokens, out_grad, routes, combine, w_gate, w_up, w_down):
    n_e = lax.axis_size("expert")
    n_x = lax.axis_size("etp")
    tok, feat = tokens.shape
    hid, width = w_gate.shape[1:]
    nq = min(CHUNKS, n_e // 2)
    ns = n_e // nq
    slots = n_e * (MAIN + 1)
    nc = feat // LANES
    vmem = pl.BlockSpec(memory_space=pltpu.VMEM)
    hbm = pl.BlockSpec(memory_space=pl.ANY)
    dma = pltpu.SemaphoreType.DMA
    grad_shape = jax.ShapeDtypeStruct((hid, width), BF16)
    outs = pl.pallas_call(
        functools.partial(kernel, n_e, n_x, nq),
        out_shape=(jax.ShapeDtypeStruct((tok, feat), BF16), grad_shape, grad_shape, grad_shape),
        in_specs=[vmem] * 4 + [hbm] * 3,
        out_specs=(vmem,) * 4,
        scratch_shapes=[
            pltpu.VMEM((hid, width), BF16),
            pltpu.VMEM((hid, width), BF16),
            pltpu.VMEM((hid, width), BF16),
            pltpu.VMEM((n_x, 2 * hid, feat), BF16),
            pltpu.VMEM((n_e, tok), F32),
            pltpu.VMEM((n_e, tok), F32),
            pltpu.VMEM((nq, tok, ns * MAIN), BF16),
            pltpu.VMEM((tok, n_e), BF16),
            pltpu.VMEM((n_e, MAIN, LANES), F32),
            pltpu.VMEM((n_e, 2 * nc + 1, MAIN, LANES), BF16),
            pltpu.VMEM((n_x, n_e, 2 * nc + 1, MAIN, LANES), BF16),
            pltpu.VMEM((ns, MAIN, LANES), F32),
            pltpu.VMEM((slots, width), BF16),
            pltpu.VMEM((slots, width), BF16),
            pltpu.VMEM((slots, hid), BF16),
            pltpu.VMEM((n_x, slots, 2 * hid), BF16),
            pltpu.VMEM((n_e, nc + 1, MAIN, LANES), BF16),
            pltpu.VMEM((n_e, nc + 1, MAIN, LANES), BF16),
            dma((3,)),
            dma((2, n_x)),
            dma((2, n_x)),
            dma((nq,)),
            dma((nq,)),
        ]
        + [dma((2, nq))] * 8
        + [dma(()), dma(())],
        compiler_params=pltpu.CompilerParams(
            collective_id=0, has_side_effects=True, vmem_limit_bytes=62 * 1024 * 1024
        ),
    )(tokens, out_grad, routes, combine, w_gate[0], w_up[0], w_down[0])
    grad_tokens, grad_gate, grad_up, grad_down = outs
    return grad_tokens, grad_gate[None], grad_up[None], grad_down[None]


def solution(mesh):
    placed = (
        P("expert", "etp"),
        P("expert", "etp"),
        P("expert", None),
        P("expert", None),
        P("expert", "etp", None),
        P("expert", "etp", None),
        P("expert", "etp", None),
    )
    return jax.shard_map(
        body,
        mesh=mesh,
        in_specs=placed,
        out_specs=(
            P("expert", "etp"),
            P("expert", "etp", None),
            P("expert", "etp", None),
            P("expert", "etp", None),
        ),
        check_vma=False,
    )
```

```python
import functools

import jax
import jax.numpy as jnp
from jax import lax
from jax.experimental import pallas as pl
from jax.experimental.pallas import tpu as pltpu
from jax.sharding import PartitionSpec as P

MESH = pl.DeviceIdType.MESH
BF16 = jnp.bfloat16
F32 = jnp.float32
LANES = 128
MAIN = 8
STRIDE = 37
CHUNKS = 8
VMEM_MIB = 48


def dot(a, b, dims=(((1,), (0,)), ((), ()))):
    return lax.dot_general(a, b, dims, preferred_element_type=F32)


LAST = (((1,), (1,)), ((), ()))
FIRST = (((0,), (0,)), ((), ()))


def kernel(
    n_e, n_x, nq,
    tokens, grads, routes, combine, wg_h, wu_h, wd_h,
    o_tok, o_gate, o_up, o_down,
    wt, place_t, weight_t, pt, pot, ovf, send, ga, gp, ovs, xs, gs,
    gu_own, h_own, ps, pr, tm, tp, y_own, ys, yr, back, ret, acc, dwo, dwp,
    wl_sem, w_s, w_r, a_s, a_r, g_s, g_r, p_s, p_r, t_s, t_r, y_s, y_r, b_s, b_r, d_s, d_r, o_sem,
):
    tok, feat = tokens.shape
    top = routes.shape[0]
    nc = feat // LANES
    hid = wg_h.shape[0]
    gu = 2 * hid
    wide = ps.shape[1]
    ns = n_e // nq
    rows = ns * (MAIN + 1)
    me = lax.axis_index("expert")
    xi = lax.axis_index("etp")
    parity = lax.rem(me, 2)
    turn = lax.rem(xi + parity, n_x)
    xa = lax.rem(turn + 1 - 2 * lax.rem(turn, 2) + n_x - parity, n_x)
    xb = lax.rem(n_x - 1 - turn + n_x - parity, n_x)
    xd = lax.rem(n_x - 1 - turn + 1 - 2 * lax.rem(n_x - 1 - turn, 2) + n_x - parity, n_x)
    on_a, on_b = {"etp": xa}, {"etp": xb}

    def remote(src, dst, s, r, dev):
        return pltpu.make_async_remote_copy(
            src_ref=src, dst_ref=dst, send_sem=s, recv_sem=r, device_id=dev, device_id_type=MESH
        )

    def drain(ref, sem):
        pltpu.make_async_copy(ref, ref, sem).wait()

    def cols_of(x):
        return pl.ds(pl.multiple_of(x * feat, LANES), feat)

    bar = pltpu.get_barrier_semaphore()
    for dev in (on_a, on_b):
        pl.semaphore_signal(bar, inc=1, device_id=dev, device_id_type=MESH)

    def greet(off, carry):
        pl.semaphore_signal(
            bar, inc=1, device_id={"expert": lax.rem(me + off, n_e)}, device_id_type=MESH
        )
        return carry

    lax.fori_loop(1, n_e, greet, 0)

    weights = (wg_h, wu_h, wd_h)
    loads = [
        pltpu.make_async_copy(
            src.at[:, cols_of(x)],
            wt.at[0, pl.ds(n * hid, hid), pl.ds(h * feat, feat)],
            wl_sem.at[n, h],
        )
        for n, src in enumerate(weights)
        for h, x in enumerate((xi, xa))
    ]
    for load in loads:
        load.start()

    label = lax.broadcasted_iota(jnp.int32, (n_e, tok), 0)
    hit = jnp.zeros((n_e, tok), F32)
    weight = jnp.zeros((n_e, tok), F32)
    for k in range(top):
        same = routes[k : k + 1, :] == label
        hit = hit + jnp.where(same, 1.0, 0.0)
        weight = weight + jnp.where(same, combine[k : k + 1, :], 0.0)
    earlier = (
        lax.broadcasted_iota(jnp.int32, (tok, tok), 0)
        < lax.broadcasted_iota(jnp.int32, (tok, tok), 1)
    )
    earlier = jnp.where(earlier, 1.0, 0.0).astype(BF16)
    place_t[...] = jnp.where(hit > 0.5, dot(hit.astype(BF16), earlier), -1.0)
    weight_t[...] = weight

    pl.semaphore_wait(bar, n_e - 1 + 2)

    swaps = [
        remote(
            src.at[:, cols_of(x)],
            wt.at[1, pl.ds(n * hid, hid), pl.ds(h * feat, feat)],
            w_s.at[n, h], w_r.at[n, h], on_b,
        )
        for n, src in enumerate(weights)
        for h, x in enumerate((xb, xd))
    ]
    for swap in swaps:
        swap.start()

    slot_id = lax.broadcasted_iota(jnp.int32, (MAIN, tok), 0).astype(F32)

    def pack(b, carry):
        base = b * ns
        hits, scales = [], []
        for u in range(ns):
            row = jnp.broadcast_to(place_t[pl.ds(base + u, 1), :], (MAIN, tok))
            wrow = jnp.broadcast_to(weight_t[pl.ds(base + u, 1), :], (MAIN, tok))
            same = row == slot_id
            hits.append(jnp.where(same, 1.0, 0.0))
            scales.append(jnp.sum(jnp.where(same, wrow, 0.0), axis=1, keepdims=True))
        pick = jnp.concatenate(hits, axis=0)
        scale = jnp.concatenate(scales, axis=0)
        pt[b] = pick.T.astype(BF16)
        pick = pick.astype(BF16)
        x = dot(pick, tokens[...])
        g = dot(pick, grads[...]) * scale
        for c in range(nc):
            cols = slice(c * LANES, (c + 1) * LANES)
            send[pl.ds(base, ns), c] = x[:, cols].reshape(ns, MAIN, LANES).astype(BF16)
            send[pl.ds(base, ns), nc + c] = g[:, cols].reshape(ns, MAIN, LANES).astype(BF16)
        return carry

    lax.fori_loop(0, nq, pack, 0)
    same = place_t[...] == float(MAIN)
    scale = jnp.sum(jnp.where(same, weight_t[...], 0.0), axis=1, keepdims=True)
    pick = jnp.where(same, 1.0, 0.0)
    pot[...] = pick.T.astype(BF16)
    pick = pick.astype(BF16)
    x = dot(pick, tokens[...])
    g = dot(pick, grads[...]) * scale
    for c in range(nc):
        cols = slice(c * LANES, (c + 1) * LANES)
        ovf[:, c, :] = x[:, cols]
        ovf[:, nc + c, :] = g[:, cols]
    send[:, 2 * nc] = ovf[...].astype(BF16)

    pltpu.make_async_copy(send.at[me], ga.at[0], a_r.at[0]).start()

    def dispatch(k, carry):
        dest = lax.rem(me + lax.rem(k * STRIDE, n_e), n_e)
        q = k // ns
        remote(send.at[dest], ga.at[k], a_s.at[q], a_r.at[q], {"expert": dest}).start()
        return carry

    lax.fori_loop(1, n_e, dispatch, 0)

    def at(q):
        return pl.ds(pl.multiple_of(q * rows, 16), rows)

    def stage1(q):
        mine = pl.ds(q * ns, ns)
        drain(ga.at[mine], a_r.at[q])
        remote(ga.at[mine], gp.at[mine], g_s.at[q], g_r.at[q], on_a).start()

    def stage2(q):
        base = q * ns
        drain(gp.at[pl.ds(base, ns)], g_r.at[q])
        main = pl.ds(pl.multiple_of(q * rows, 16), ns * MAIN)
        over = pl.ds(pl.multiple_of(q * rows + ns * MAIN, 16), ns)
        for j, buf in enumerate((ga, gp)):
            ovs[...] = buf[pl.ds(base, ns), 2 * nc].astype(F32)
            for c in range(nc):
                cols = slice(j * feat + c * LANES, j * feat + (c + 1) * LANES)
                xs[main, cols] = buf[pl.ds(base, ns), c].reshape(ns * MAIN, LANES)
                gs[main, cols] = buf[pl.ds(base, ns), nc + c].reshape(ns * MAIN, LANES)
                xs[over, cols] = ovs[:, c, :].astype(BF16)
                gs[over, cols] = ovs[:, nc + c, :].astype(BF16)
        x = xs[at(q), :]
        g = gs[at(q), :]
        ps[at(q), :gu] = dot(x, wt[1, :gu], LAST).astype(BF16)
        part = dot(g, wt[1, gu:], LAST)
        pad = jnp.zeros((rows, wide - gu - hid), F32)
        ps[at(q), gu:] = jnp.concatenate([part, pad], axis=1).astype(BF16)
        remote(ps.at[at(q)], pr.at[at(q)], p_s.at[q], p_r.at[q], on_b).start()
        gu_own[at(q), :] = dot(x, wt[0, :gu], LAST)
        h_own[at(q), :] = dot(g, wt[0, gu:], LAST)

    def stage3(q):
        drain(pr.at[at(q)], p_r.at[q])
        both = gu_own[at(q), :] + pr[at(q), :gu].astype(F32)
        hidden = h_own[at(q), :] + pr[at(q), gu : gu + hid].astype(F32)
        gate = both[:, :hid]
        up = both[:, hid:]
        sigma = jax.nn.sigmoid(gate)
        silu = gate * sigma
        gate_term = hidden * up * sigma * (1.0 + gate * (1.0 - sigma))
        up_term = hidden * silu
        tm[at(q), :gu] = jnp.concatenate([gate_term, up_term], axis=1).astype(BF16)
        pad = jnp.zeros((rows, wide - gu - hid), F32)
        tm[at(q), gu:] = jnp.concatenate([silu * up, pad], axis=1).astype(BF16)
        remote(tm.at[at(q)], tp.at[at(q)], t_s.at[q], t_r.at[q], on_b).start()

    def stage4(q):
        drain(tp.at[at(q)], t_r.at[q])
        mine = tm[at(q), :gu]
        theirs = tp[at(q), :gu]
        part = dot(mine, wt[0, :gu, feat:]) + dot(theirs, wt[1, :gu, feat:])
        ys[at(q), :] = part.astype(BF16)
        remote(ys.at[at(q)], yr.at[at(q)], y_s.at[q], y_r.at[q], on_a).start()
        y_own[at(q), :] = dot(mine, wt[0, :gu, :feat]) + dot(theirs, wt[1, :gu, :feat])

    def stage5(q):
        base = q * ns
        drain(yr.at[at(q)], y_r.at[q])
        slot = y_own[at(q), :] + yr[at(q), :].astype(F32)
        ovs[...] = jnp.zeros_like(ovs)
        for c in range(nc):
            cols = slice(c * LANES, (c + 1) * LANES)
            main = slot[: ns * MAIN, cols].reshape(ns, MAIN, LANES)
            back[pl.ds(base, ns), c] = main.astype(BF16)
            ovs[:, c, :] = slot[ns * MAIN :, cols]
        back[pl.ds(base, ns), nc] = ovs[...].astype(BF16)

        @pl.when(q == 0)
        def _():
            pltpu.make_async_copy(back.at[0], ret.at[me], b_r).start()

        def answer(k, carry):
            dest = lax.rem(me + n_e - lax.rem(k * STRIDE, n_e), n_e)
            remote(back.at[k], ret.at[me], b_s, b_r, {"expert": dest}).start()
            return carry

        lax.fori_loop(jnp.maximum(base, 1), base + ns, answer, 0)

    last = nq - max(1, nq // 4)
    middle = (last + 1) // 2
    ranges = [(0, middle), (middle, last)] if middle < last else [(0, last)]

    def weight_grads(block, first, stop):
        r = slice(first * rows, stop * rows)
        t = (tm, tp)[block]
        return dot(t[r, :gu], xs[r, :], FIRST), dot(t[r, gu : gu + hid], gs[r, :], FIRST)

    def step(t, carry):
        for lag, stage in enumerate((stage1, stage2, stage3, stage4, stage5)):
            q = t - lag
            if stage is stage2:

                @pl.when(q == 0)
                def _():
                    for load in loads:
                        load.wait()
                    for swap in swaps:
                        swap.wait_recv()

            @pl.when(jnp.logical_and(q >= 0, q < nq))
            def _():
                stage(q)

        for n, (first, stop) in enumerate(ranges):

            @pl.when(t - 3 == stop - 1)
            def _():
                for block in range(2):
                    both, down = weight_grads(block, first, stop)
                    if n == 0:
                        acc[block, :gu] = both
                        acc[block, gu:] = down
                    else:
                        acc[block, :gu] += both
                        acc[block, gu:] += down

        return carry

    lax.fori_loop(0, nq + 4, step, 0)

    outs = (o_gate, o_up, o_down)

    def piece(ref, n, h):
        return ref.at[pl.ds(n * hid, hid), pl.ds(h * feat, feat)]

    both, down = weight_grads(1, last, nq)
    dwp[:gu] = (acc[1, :gu] + both).astype(BF16)
    dwp[gu:] = (acc[1, gu:] + down).astype(BF16)
    theirs = [
        remote(
            piece(dwp, n, h), out.at[:, cols_of(x)], d_s.at[n, h], d_r.at[n, h], on_b
        )
        for n, out in enumerate(outs)
        for h, x in enumerate((xi, xa))
    ]
    for copy in theirs:
        copy.start()
    both, down = weight_grads(0, last, nq)
    dwo[:gu] = (acc[0, :gu] + both).astype(BF16)
    dwo[gu:] = (acc[0, gu:] + down).astype(BF16)
    mine = [
        pltpu.make_async_copy(piece(dwo, n, h), out.at[:, cols_of(x)], o_sem.at[n, h])
        for n, out in enumerate(outs)
        for h, x in enumerate((xi, xa))
    ]
    for copy in mine:
        copy.start()

    drain(ret, b_r)
    ovf[...] = ret[:, nc].astype(F32)
    for c in range(nc):
        total = dot(pot[...], ovf[:, c, :].astype(BF16))
        for b in range(nq):
            part = ret[pl.ds(b * ns, ns), c].reshape(ns * MAIN, LANES)
            total = total + dot(pt[b], part)
        o_tok[:, c * LANES : (c + 1) * LANES] = total.astype(BF16)

    for swap in swaps:
        swap.wait_send()
    drain(back.at[pl.ds(1, n_e - 1)], b_s)
    drain(send.at[pl.ds(0, ns - 1)], a_s.at[0])

    def flush_a(q, carry):
        drain(send.at[pl.ds(0, ns)], a_s.at[q])
        return carry

    lax.fori_loop(1, nq, flush_a, 0)

    def flush(q, carry):
        drain(ga.at[pl.ds(q * ns, ns)], g_s.at[q])
        drain(ps.at[at(q)], p_s.at[q])
        drain(tm.at[at(q)], t_s.at[q])
        drain(ys.at[at(q)], y_s.at[q])
        return carry

    lax.fori_loop(0, nq, flush, 0)
    for copy in mine:
        copy.wait()
    for copy in theirs:
        copy.wait_send()
        copy.wait_recv()


def body(tokens, out_grad, routes, combine, w_gate, w_up, w_down):
    n_e = lax.axis_size("expert")
    n_x = lax.axis_size("etp")
    tok, feat = tokens.shape
    hid, width = w_gate.shape[1:]
    nq = min(CHUNKS, n_e // 2)
    ns = n_e // nq
    slots = n_e * (MAIN + 1)
    nc = feat // LANES
    two = 2 * feat
    wide = (3 * hid + LANES - 1) // LANES * LANES
    vmem = pl.BlockSpec(memory_space=pltpu.VMEM)
    hbm = pl.BlockSpec(memory_space=pl.ANY)
    dma = pltpu.SemaphoreType.DMA
    grad_shape = jax.ShapeDtypeStruct((hid, width), BF16)
    outs = pl.pallas_call(
        functools.partial(kernel, n_e, n_x, nq),
        out_shape=(jax.ShapeDtypeStruct((tok, feat), BF16), grad_shape, grad_shape, grad_shape),
        in_specs=[vmem] * 4 + [hbm] * 3,
        out_specs=(vmem, hbm, hbm, hbm),
        scratch_shapes=[
            pltpu.VMEM((2, 3 * hid, two), BF16),
            pltpu.VMEM((n_e, tok), F32),
            pltpu.VMEM((n_e, tok), F32),
            pltpu.VMEM((nq, tok, ns * MAIN), BF16),
            pltpu.VMEM((tok, n_e), BF16),
            pltpu.VMEM((n_e, MAIN, LANES), F32),
            pltpu.VMEM((n_e, 2 * nc + 1, MAIN, LANES), BF16),
            pltpu.VMEM((n_e, 2 * nc + 1, MAIN, LANES), BF16),
            pltpu.VMEM((n_e, 2 * nc + 1, MAIN, LANES), BF16),
            pltpu.VMEM((ns, MAIN, LANES), F32),
            pltpu.VMEM((slots, two), BF16),
            pltpu.VMEM((slots, two), BF16),
            pltpu.VMEM((slots, 2 * hid), F32),
            pltpu.VMEM((slots, hid), F32),
            pltpu.VMEM((slots, wide), BF16),
            pltpu.VMEM((slots, wide), BF16),
            pltpu.VMEM((slots, wide), BF16),
            pltpu.VMEM((slots, wide), BF16),
            pltpu.VMEM((slots, feat), F32),
            pltpu.VMEM((slots, feat), BF16),
            pltpu.VMEM((slots, feat), BF16),
            pltpu.VMEM((n_e, nc + 1, MAIN, LANES), BF16),
            pltpu.VMEM((n_e, nc + 1, MAIN, LANES), BF16),
            pltpu.VMEM((2, 3 * hid, two), F32),
            pltpu.VMEM((3 * hid, two), BF16),
            pltpu.VMEM((3 * hid, two), BF16),
            dma((3, 2)),
            dma((3, 2)),
            dma((3, 2)),
        ]
        + [dma((nq,))] * 10
        + [dma(()), dma(()), dma((3, 2)), dma((3, 2)), dma((3, 2))],
        compiler_params=pltpu.CompilerParams(
            collective_id=0, has_side_effects=True, vmem_limit_bytes=VMEM_MIB * 1024 * 1024
        ),
    )(tokens, out_grad, routes.T, combine.T, w_gate[0], w_up[0], w_down[0])
    grad_tokens, grad_gate, grad_up, grad_down = outs
    return grad_tokens, grad_gate[None], grad_up[None], grad_down[None]


def solution(mesh):
    placed = (
        P("expert", "etp"),
        P("expert", "etp"),
        P("expert", None),
        P("expert", None),
        P("expert", "etp", None),
        P("expert", "etp", None),
        P("expert", "etp", None),
    )
    return jax.shard_map(
        body,
        mesh=mesh,
        in_specs=placed,
        out_specs=(
            P("expert", "etp"),
            P("expert", "etp", None),
            P("expert", "etp", None),
            P("expert", "etp", None),
        ),
        check_vma=False,
    )
```

```python
import functools

import jax
import jax.numpy as jnp
from jax import lax
from jax.experimental import pallas as pl
from jax.experimental.pallas import tpu as pltpu
from jax.sharding import PartitionSpec as P

MESH = pl.DeviceIdType.MESH
BF16 = jnp.bfloat16
F32 = jnp.float32
LANES = 128
MAIN = 8
STRIDE = 37
SPAN = 8
CHUNKS = 8
VMEM_MIB = 48


def dot(a, b, dims=(((1,), (0,)), ((), ()))):
    return lax.dot_general(a, b, dims, preferred_element_type=F32)


LAST = (((1,), (1,)), ((), ()))
FIRST = (((0,), (0,)), ((), ()))


def kernel(
    n_e, n_x, nq,
    tok_h, grad_h, route_h, comb_h, wg_h, wu_h, wd_h,
    o_tok, o_gate, o_up, o_down,
    tokens, grads, routes, combine, wt, place_t, weight_t, pk, wk, pt, pot, ovf, send, ga, gp, ovs, xs, gs,
    gu_own, h_own, ps, pr, tm, tp, y_own, ys, yr, back, ret, acc, dwo, dwp,
    in_sem, wl_sem, w_s, w_r, a_s, a_r, g_s, g_r, p_s, p_r, t_s, t_r, y_s, y_r, b_s, b_r, d_s, d_r, o_sem,
):
    tok, feat = tokens.shape
    top = routes.shape[0]
    nc = feat // LANES
    hid = wg_h.shape[0]
    gu = 2 * hid
    wide = ps.shape[1]
    ns = n_e // nq
    rows = ns * (MAIN + 1)
    me = lax.axis_index("expert")
    xi = lax.axis_index("etp")
    parity = lax.rem(me, 2)
    turn = lax.rem(xi + parity, n_x)
    xa = lax.rem(turn + 1 - 2 * lax.rem(turn, 2) + n_x - parity, n_x)
    xb = lax.rem(n_x - 1 - turn + n_x - parity, n_x)
    xd = lax.rem(n_x - 1 - turn + 1 - 2 * lax.rem(n_x - 1 - turn, 2) + n_x - parity, n_x)
    on_a, on_b = {"etp": xa}, {"etp": xb}

    def remote(src, dst, s, r, dev):
        return pltpu.make_async_remote_copy(
            src_ref=src, dst_ref=dst, send_sem=s, recv_sem=r, device_id=dev, device_id_type=MESH
        )

    def drain(ref, sem):
        pltpu.make_async_copy(ref, ref, sem).wait()

    def cols_of(x):
        return pl.ds(pl.multiple_of(x * feat, LANES), feat)

    span = min(SPAN, n_e // 2)
    layers = n_e // (2 * span)

    def partner(k, ahead):
        m = lax.rem(k * STRIDE, n_e)
        step_c, step_y, step_z = lax.rem(m, 2), lax.rem(m // 2, span), m // (2 * span)
        if not ahead:
            step_c, step_y, step_z = 2 - step_c, span - step_y, layers - step_z
        z = lax.rem(me // (2 * span) + step_z, layers)
        y = lax.rem(lax.rem(me // 2, span) + step_y, span)
        return (z * span + y) * 2 + lax.rem(lax.rem(me, 2) + step_c, 2)

    reads = [
        pltpu.make_async_copy(src, dst, in_sem.at[n])
        for n, (src, dst) in enumerate(
            ((route_h, routes), (comb_h, combine), (tok_h, tokens), (grad_h, grads))
        )
    ]
    for read in reads:
        read.start()

    bar = pltpu.get_barrier_semaphore()
    for dev in (on_a, on_b):
        pl.semaphore_signal(bar, inc=1, device_id=dev, device_id_type=MESH)

    def greet(off, carry):
        pl.semaphore_signal(
            bar, inc=1, device_id={"expert": lax.rem(me + off, n_e)}, device_id_type=MESH
        )
        return carry

    lax.fori_loop(1, n_e, greet, 0)

    weights = (wg_h, wu_h, wd_h)
    loads = [
        pltpu.make_async_copy(
            src.at[:, cols_of(x)],
            wt.at[0, pl.ds(n * hid, hid), pl.ds(h * feat, feat)],
            wl_sem.at[n, h],
        )
        for n, src in enumerate(weights)
        for h, x in enumerate((xi, xa))
    ]
    for load in loads:
        load.start()

    for read in reads:
        read.wait()
    label = lax.broadcasted_iota(jnp.int32, (n_e, tok), 0)
    hit = jnp.zeros((n_e, tok), F32)
    weight = jnp.zeros((n_e, tok), F32)
    for k in range(top):
        same = routes[k : k + 1, :] == label
        hit = hit + jnp.where(same, 1.0, 0.0)
        weight = weight + jnp.where(same, combine[k : k + 1, :], 0.0)
    earlier = (
        lax.broadcasted_iota(jnp.int32, (tok, tok), 0)
        < lax.broadcasted_iota(jnp.int32, (tok, tok), 1)
    )
    earlier = jnp.where(earlier, 1.0, 0.0).astype(BF16)
    place_t[...] = jnp.where(hit > 0.5, dot(hit.astype(BF16), earlier), -1.0)
    weight_t[...] = weight

    pl.semaphore_wait(bar, n_e - 1 + 2)

    swaps = [
        remote(
            src.at[:, cols_of(x)],
            wt.at[1, pl.ds(n * hid, hid), pl.ds(h * feat, feat)],
            w_s.at[n, h], w_r.at[n, h], on_b,
        )
        for n, src in enumerate(weights)
        for h, x in enumerate((xb, xd))
    ]
    for swap in swaps:
        swap.start()

    slot_id = lax.broadcasted_iota(jnp.int32, (MAIN, tok), 0).astype(F32)

    def pack(q, carry):
        base = q * ns
        hits, scales = [], []
        for u in range(ns):
            e = partner(base + u, True)
            pk[pl.ds(base + u, 1), :] = place_t[pl.ds(e, 1), :]
            wk[pl.ds(base + u, 1), :] = weight_t[pl.ds(e, 1), :]
            row = jnp.broadcast_to(place_t[pl.ds(e, 1), :], (MAIN, tok))
            wrow = jnp.broadcast_to(weight_t[pl.ds(e, 1), :], (MAIN, tok))
            same = row == slot_id
            hits.append(jnp.where(same, 1.0, 0.0))
            scales.append(jnp.sum(jnp.where(same, wrow, 0.0), axis=1, keepdims=True))
        chunk = pl.ds(base, ns)
        ninth = pk[chunk, :] == float(MAIN)
        scale = jnp.sum(jnp.where(ninth, wk[chunk, :], 0.0), axis=1, keepdims=True)
        pick = jnp.where(ninth, 1.0, 0.0).astype(BF16)
        x = dot(pick, tokens[...])
        g = dot(pick, grads[...]) * scale
        for c in range(nc):
            cols = slice(c * LANES, (c + 1) * LANES)
            ovs[:, c, :] = x[:, cols]
            ovs[:, nc + c, :] = g[:, cols]
        send[chunk, 2 * nc] = ovs[...].astype(BF16)
        pick = jnp.concatenate(hits, axis=0)
        scale = jnp.concatenate(scales, axis=0)
        pt[q] = pick.T.astype(BF16)
        pick = pick.astype(BF16)
        x = dot(pick, tokens[...])
        g = dot(pick, grads[...]) * scale
        for c in range(nc):
            cols = slice(c * LANES, (c + 1) * LANES)
            send[chunk, c] = x[:, cols].reshape(ns, MAIN, LANES).astype(BF16)
            send[chunk, nc + c] = g[:, cols].reshape(ns, MAIN, LANES).astype(BF16)

        @pl.when(q == 0)
        def _():
            pltpu.make_async_copy(send.at[0], ga.at[0], a_r.at[0]).start()

        def dispatch(k, carry):
            dev = {"expert": partner(k, True)}
            remote(send.at[k], ga.at[k], a_s.at[q], a_r.at[q], dev).start()
            return carry

        lax.fori_loop(jnp.maximum(base, 1), base + ns, dispatch, 0)
        return carry

    lax.fori_loop(0, nq, pack, 0)
    pot[...] = jnp.where(pk[...] == float(MAIN), 1.0, 0.0).T.astype(BF16)

    def at(q):
        return pl.ds(pl.multiple_of(q * rows, 16), rows)

    def stage1(q):
        mine = pl.ds(q * ns, ns)
        drain(ga.at[mine], a_r.at[q])
        remote(ga.at[mine], gp.at[mine], g_s.at[q], g_r.at[q], on_a).start()

    def stage2(q):
        base = q * ns
        drain(gp.at[pl.ds(base, ns)], g_r.at[q])
        main = pl.ds(pl.multiple_of(q * rows, 16), ns * MAIN)
        over = pl.ds(pl.multiple_of(q * rows + ns * MAIN, 16), ns)
        for j, buf in enumerate((ga, gp)):
            ovs[...] = buf[pl.ds(base, ns), 2 * nc].astype(F32)
            for c in range(nc):
                cols = slice(j * feat + c * LANES, j * feat + (c + 1) * LANES)
                xs[main, cols] = buf[pl.ds(base, ns), c].reshape(ns * MAIN, LANES)
                gs[main, cols] = buf[pl.ds(base, ns), nc + c].reshape(ns * MAIN, LANES)
                xs[over, cols] = ovs[:, c, :].astype(BF16)
                gs[over, cols] = ovs[:, nc + c, :].astype(BF16)
        x = xs[at(q), :]
        g = gs[at(q), :]
        ps[at(q), :gu] = dot(x, wt[1, :gu], LAST).astype(BF16)
        part = dot(g, wt[1, gu:], LAST)
        pad = jnp.zeros((rows, wide - gu - hid), F32)
        ps[at(q), gu:] = jnp.concatenate([part, pad], axis=1).astype(BF16)
        remote(ps.at[at(q)], pr.at[at(q)], p_s.at[q], p_r.at[q], on_b).start()
        gu_own[at(q), :] = dot(x, wt[0, :gu], LAST)
        h_own[at(q), :] = dot(g, wt[0, gu:], LAST)

    def stage3(q):
        drain(pr.at[at(q)], p_r.at[q])
        both = gu_own[at(q), :] + pr[at(q), :gu].astype(F32)
        hidden = h_own[at(q), :] + pr[at(q), gu : gu + hid].astype(F32)
        gate = both[:, :hid]
        up = both[:, hid:]
        sigma = jax.nn.sigmoid(gate)
        silu = gate * sigma
        gate_term = hidden * up * sigma * (1.0 + gate * (1.0 - sigma))
        up_term = hidden * silu
        tm[at(q), :gu] = jnp.concatenate([gate_term, up_term], axis=1).astype(BF16)
        pad = jnp.zeros((rows, wide - gu - hid), F32)
        tm[at(q), gu:] = jnp.concatenate([silu * up, pad], axis=1).astype(BF16)
        remote(tm.at[at(q)], tp.at[at(q)], t_s.at[q], t_r.at[q], on_b).start()

    def stage4(q):
        drain(tp.at[at(q)], t_r.at[q])
        mine = tm[at(q), :gu]
        theirs = tp[at(q), :gu]
        part = dot(mine, wt[0, :gu, feat:]) + dot(theirs, wt[1, :gu, feat:])
        ys[at(q), :] = part.astype(BF16)
        remote(ys.at[at(q)], yr.at[at(q)], y_s.at[q], y_r.at[q], on_a).start()
        y_own[at(q), :] = dot(mine, wt[0, :gu, :feat]) + dot(theirs, wt[1, :gu, :feat])

    def stage5(q):
        base = q * ns
        drain(yr.at[at(q)], y_r.at[q])
        slot = y_own[at(q), :] + yr[at(q), :].astype(F32)
        ovs[...] = jnp.zeros_like(ovs)
        for c in range(nc):
            cols = slice(c * LANES, (c + 1) * LANES)
            main = slot[: ns * MAIN, cols].reshape(ns, MAIN, LANES)
            back[pl.ds(base, ns), c] = main.astype(BF16)
            ovs[:, c, :] = slot[ns * MAIN :, cols]
        back[pl.ds(base, ns), nc] = ovs[...].astype(BF16)

        @pl.when(q == 0)
        def _():
            pltpu.make_async_copy(back.at[0], ret.at[0], b_r.at[0]).start()

        def answer(k, carry):
            dev = {"expert": partner(k, False)}
            remote(back.at[k], ret.at[k], b_s, b_r.at[q], dev).start()
            return carry

        lax.fori_loop(jnp.maximum(base, 1), base + ns, answer, 0)

    last = nq - 1
    middle = (last + 1) // 2
    ranges = [(0, middle), (middle, last)] if middle < last else [(0, last)]

    def weight_grads(block, first, stop):
        r = slice(first * rows, stop * rows)
        t = (tm, tp)[block]
        return dot(t[r, :gu], xs[r, :], FIRST), dot(t[r, gu : gu + hid], gs[r, :], FIRST)

    def step(t, carry):
        for lag, stage in enumerate((stage1, stage2, stage3, stage4, stage5)):
            q = t - lag
            if stage is stage2:

                @pl.when(q == 0)
                def _():
                    for load in loads:
                        load.wait()
                    for swap in swaps:
                        swap.wait_recv()

            @pl.when(jnp.logical_and(q >= 0, q < nq))
            def _():
                stage(q)

        for n, (first, stop) in enumerate(ranges):

            @pl.when(t - 3 == stop - 1)
            def _():
                for block in range(2):
                    both, down = weight_grads(block, first, stop)
                    if n == 0:
                        acc[block, :gu] = both
                        acc[block, gu:] = down
                    else:
                        acc[block, :gu] += both
                        acc[block, gu:] += down

        return carry

    lax.fori_loop(0, nq + 3, step, 0)

    outs = (o_gate, o_up, o_down)

    def piece(ref, n, h):
        return ref.at[pl.ds(n * hid, hid), pl.ds(h * feat, feat)]

    both, down = weight_grads(1, last, nq)
    dwp[:gu] = (acc[1, :gu] + both).astype(BF16)
    dwp[gu:] = (acc[1, gu:] + down).astype(BF16)
    theirs = [
        remote(
            piece(dwp, n, h), out.at[:, cols_of(x)], d_s.at[n, h], d_r.at[n, h], on_b
        )
        for n, out in enumerate(outs)
        for h, x in enumerate((xi, xa))
    ]
    for copy in theirs:
        copy.start()
    stage5(nq - 1)
    both, down = weight_grads(0, last, nq)
    dwo[:gu] = (acc[0, :gu] + both).astype(BF16)
    dwo[gu:] = (acc[0, gu:] + down).astype(BF16)
    mine = [
        pltpu.make_async_copy(piece(dwo, n, h), out.at[:, cols_of(x)], o_sem.at[n, h])
        for n, out in enumerate(outs)
        for h, x in enumerate((xi, xa))
    ]
    for copy in mine:
        copy.start()

    total = [jnp.zeros((tok, LANES), F32) for c in range(nc)]
    for q in range(nq):
        chunk = slice(q * ns, (q + 1) * ns)
        drain(ret.at[chunk], b_r.at[q])
        for c in range(nc):
            total[c] = total[c] + dot(pt[q], ret[chunk, c].reshape(ns * MAIN, LANES))
    ovf[...] = ret[:, nc].astype(F32)
    for c in range(nc):
        total[c] = total[c] + dot(pot[...], ovf[:, c, :].astype(BF16))
        o_tok[:, c * LANES : (c + 1) * LANES] = total[c].astype(BF16)

    for swap in swaps:
        swap.wait_send()
    drain(back.at[pl.ds(1, n_e - 1)], b_s)
    drain(send.at[pl.ds(0, ns - 1)], a_s.at[0])

    def flush_a(q, carry):
        drain(send.at[pl.ds(0, ns)], a_s.at[q])
        return carry

    lax.fori_loop(1, nq, flush_a, 0)

    def flush(q, carry):
        drain(ga.at[pl.ds(q * ns, ns)], g_s.at[q])
        drain(ps.at[at(q)], p_s.at[q])
        drain(tm.at[at(q)], t_s.at[q])
        drain(ys.at[at(q)], y_s.at[q])
        return carry

    lax.fori_loop(0, nq, flush, 0)
    for copy in mine:
        copy.wait()
    for copy in theirs:
        copy.wait_send()
        copy.wait_recv()


def body(tokens, out_grad, routes, combine, w_gate, w_up, w_down):
    n_e = lax.axis_size("expert")
    n_x = lax.axis_size("etp")
    tok, feat = tokens.shape
    hid, width = w_gate.shape[1:]
    nq = min(CHUNKS, n_e // 2)
    ns = n_e // nq
    slots = n_e * (MAIN + 1)
    nc = feat // LANES
    two = 2 * feat
    wide = (3 * hid + LANES - 1) // LANES * LANES
    vmem = pl.BlockSpec(memory_space=pltpu.VMEM)
    hbm = pl.BlockSpec(memory_space=pl.ANY)
    dma = pltpu.SemaphoreType.DMA
    grad_shape = jax.ShapeDtypeStruct((hid, width), BF16)
    outs = pl.pallas_call(
        functools.partial(kernel, n_e, n_x, nq),
        out_shape=(jax.ShapeDtypeStruct((tok, feat), BF16), grad_shape, grad_shape, grad_shape),
        in_specs=[pl.BlockSpec(memory_space=pltpu.HBM)] * 7,
        out_specs=(vmem, hbm, hbm, hbm),
        scratch_shapes=[
            pltpu.VMEM((tok, feat), BF16),
            pltpu.VMEM((tok, feat), BF16),
            pltpu.VMEM((routes.shape[1], tok), jnp.int32),
            pltpu.VMEM((routes.shape[1], tok), F32),
            pltpu.VMEM((2, 3 * hid, two), BF16),
            pltpu.VMEM((n_e, tok), F32),
            pltpu.VMEM((n_e, tok), F32),
            pltpu.VMEM((n_e, tok), F32),
            pltpu.VMEM((n_e, tok), F32),
            pltpu.VMEM((nq, tok, ns * MAIN), BF16),
            pltpu.VMEM((tok, n_e), BF16),
            pltpu.VMEM((n_e, MAIN, LANES), F32),
            pltpu.VMEM((n_e, 2 * nc + 1, MAIN, LANES), BF16),
            pltpu.VMEM((n_e, 2 * nc + 1, MAIN, LANES), BF16),
            pltpu.VMEM((n_e, 2 * nc + 1, MAIN, LANES), BF16),
            pltpu.VMEM((ns, MAIN, LANES), F32),
            pltpu.VMEM((slots, two), BF16),
            pltpu.VMEM((slots, two), BF16),
            pltpu.VMEM((slots, 2 * hid), F32),
            pltpu.VMEM((slots, hid), F32),
            pltpu.VMEM((slots, wide), BF16),
            pltpu.VMEM((slots, wide), BF16),
            pltpu.VMEM((slots, wide), BF16),
            pltpu.VMEM((slots, wide), BF16),
            pltpu.VMEM((slots, feat), F32),
            pltpu.VMEM((slots, feat), BF16),
            pltpu.VMEM((slots, feat), BF16),
            pltpu.VMEM((n_e, nc + 1, MAIN, LANES), BF16),
            pltpu.VMEM((n_e, nc + 1, MAIN, LANES), BF16),
            pltpu.VMEM((2, 3 * hid, two), F32),
            pltpu.VMEM((3 * hid, two), BF16),
            pltpu.VMEM((3 * hid, two), BF16),
            dma((4,)),
            dma((3, 2)),
            dma((3, 2)),
            dma((3, 2)),
        ]
        + [dma((nq,))] * 10
        + [dma(()), dma((nq,)), dma((3, 2)), dma((3, 2)), dma((3, 2))],
        compiler_params=pltpu.CompilerParams(
            collective_id=0, has_side_effects=True, vmem_limit_bytes=VMEM_MIB * 1024 * 1024
        ),
    )(*[pltpu.with_memory_space_constraint(a, pltpu.HBM) for a in (tokens, out_grad, routes.T, combine.T, w_gate[0], w_up[0], w_down[0])])
    grad_tokens, grad_gate, grad_up, grad_down = outs
    return grad_tokens, grad_gate[None], grad_up[None], grad_down[None]


def solution(mesh):
    placed = (
        P("expert", "etp"),
        P("expert", "etp"),
        P("expert", None),
        P("expert", None),
        P("expert", "etp", None),
        P("expert", "etp", None),
        P("expert", "etp", None),
    )
    return jax.shard_map(
        body,
        mesh=mesh,
        in_specs=placed,
        out_specs=(
            P("expert", "etp"),
            P("expert", "etp", None),
            P("expert", "etp", None),
            P("expert", "etp", None),
        ),
        check_vma=False,
    )
```

```python
import functools

import jax
import jax.numpy as jnp
from jax import lax
from jax.experimental import pallas as pl
from jax.experimental.pallas import tpu as pltpu
from jax.sharding import PartitionSpec as P

MESH = pl.DeviceIdType.MESH
BF16 = jnp.bfloat16
F32 = jnp.float32
LANES = 128
MAIN = 8
STRIDE = 3
SPAN = 8
CHUNKS = 8
VMEM_MIB = 48


def dot(a, b, dims=(((1,), (0,)), ((), ()))):
    return lax.dot_general(a, b, dims, preferred_element_type=F32)


LAST = (((1,), (1,)), ((), ()))
FIRST = (((0,), (0,)), ((), ()))


def kernel(
    n_e, n_x, nq,
    tok_h, grad_h, route_h, comb_h, wg_h, wu_h, wd_h,
    o_tok, o_gate, o_up, o_down,
    tokens, grads, routes, combine, wt, place_t, weight_t, pk, wk, pt, pot, ovf, send, ga, gp, ovs, xs, gs,
    gu_own, h_own, ps, pr, tm, tp, y_own, ys, yr, back, ret, acc, dwo, dwp,
    in_sem, wl_sem, w_s, w_r, a_s, a_r, g_s, g_r, p_s, p_r, t_s, t_r, y_s, y_r, b_s, b_r, d_s, d_r, o_sem,
):
    tok, feat = tokens.shape
    top = routes.shape[0]
    nc = feat // LANES
    hid = wg_h.shape[0]
    gu = 2 * hid
    wide = ps.shape[1]
    ns = n_e // nq
    rows = ns * (MAIN + 1)
    me = lax.axis_index("expert")
    xi = lax.axis_index("etp")
    parity = lax.rem(me, 2)
    turn = lax.rem(xi + parity, n_x)
    xa = lax.rem(turn + 1 - 2 * lax.rem(turn, 2) + n_x - parity, n_x)
    xb = lax.rem(n_x - 1 - turn + n_x - parity, n_x)
    xd = lax.rem(n_x - 1 - turn + 1 - 2 * lax.rem(n_x - 1 - turn, 2) + n_x - parity, n_x)
    on_a, on_b = {"etp": xa}, {"etp": xb}

    def remote(src, dst, s, r, dev):
        return pltpu.make_async_remote_copy(
            src_ref=src, dst_ref=dst, send_sem=s, recv_sem=r, device_id=dev, device_id_type=MESH
        )

    def drain(ref, sem):
        pltpu.make_async_copy(ref, ref, sem).wait()

    def cols_of(x):
        return pl.ds(pl.multiple_of(x * feat, LANES), feat)

    span = min(SPAN, n_e // 2)
    layers = n_e // (2 * span)

    def partner(k, ahead):
        lo, hi = lax.rem(k, 2 * span), k // (2 * span)
        step_c = lo // span
        step_y = lax.rem(lo * STRIDE, span)
        step_z = lax.rem(step_y + hi, layers)
        if not ahead:
            step_c, step_y, step_z = 2 - step_c, span - step_y, layers - step_z
        z = lax.rem(me // (2 * span) + step_z, layers)
        y = lax.rem(lax.rem(me // 2, span) + step_y, span)
        return (z * span + y) * 2 + lax.rem(lax.rem(me, 2) + step_c, 2)

    reads = [
        pltpu.make_async_copy(src, dst, in_sem.at[n])
        for n, (src, dst) in enumerate(
            ((route_h, routes), (comb_h, combine), (tok_h, tokens), (grad_h, grads))
        )
    ]
    for read in reads:
        read.start()

    bar = pltpu.get_barrier_semaphore()
    for dev in (on_a, on_b):
        pl.semaphore_signal(bar, inc=1, device_id=dev, device_id_type=MESH)

    def greet(off, carry):
        pl.semaphore_signal(
            bar, inc=1, device_id={"expert": lax.rem(me + off, n_e)}, device_id_type=MESH
        )
        return carry

    lax.fori_loop(1, n_e, greet, 0)

    weights = (wg_h, wu_h, wd_h)
    loads = [
        pltpu.make_async_copy(
            src.at[:, cols_of(x)],
            wt.at[0, pl.ds(n * hid, hid), pl.ds(h * feat, feat)],
            wl_sem.at[n, h],
        )
        for n, src in enumerate(weights)
        for h, x in enumerate((xi, xa))
    ]
    for load in loads:
        load.start()

    for read in reads:
        read.wait()
    label = lax.broadcasted_iota(jnp.int32, (n_e, tok), 0)
    hit = jnp.zeros((n_e, tok), F32)
    weight = jnp.zeros((n_e, tok), F32)
    for k in range(top):
        same = routes[k : k + 1, :] == label
        hit = hit + jnp.where(same, 1.0, 0.0)
        weight = weight + jnp.where(same, combine[k : k + 1, :], 0.0)
    earlier = (
        lax.broadcasted_iota(jnp.int32, (tok, tok), 0)
        < lax.broadcasted_iota(jnp.int32, (tok, tok), 1)
    )
    earlier = jnp.where(earlier, 1.0, 0.0).astype(BF16)
    place_t[...] = jnp.where(hit > 0.5, dot(hit.astype(BF16), earlier), -1.0)
    weight_t[...] = weight

    pl.semaphore_wait(bar, n_e - 1 + 2)

    swaps = [
        remote(
            src.at[:, cols_of(x)],
            wt.at[1, pl.ds(n * hid, hid), pl.ds(h * feat, feat)],
            w_s.at[n, h], w_r.at[n, h], on_b,
        )
        for n, src in enumerate(weights)
        for h, x in enumerate((xb, xd))
    ]
    for swap in swaps:
        swap.start()

    slot_id = lax.broadcasted_iota(jnp.int32, (MAIN, tok), 0).astype(F32)

    def pack(q, carry):
        base = q * ns
        hits, scales = [], []
        for u in range(ns):
            e = partner(base + u, True)
            pk[pl.ds(base + u, 1), :] = place_t[pl.ds(e, 1), :]
            wk[pl.ds(base + u, 1), :] = weight_t[pl.ds(e, 1), :]
            row = jnp.broadcast_to(place_t[pl.ds(e, 1), :], (MAIN, tok))
            wrow = jnp.broadcast_to(weight_t[pl.ds(e, 1), :], (MAIN, tok))
            same = row == slot_id
            hits.append(jnp.where(same, 1.0, 0.0))
            scales.append(jnp.sum(jnp.where(same, wrow, 0.0), axis=1, keepdims=True))
        chunk = pl.ds(base, ns)
        ninth = pk[chunk, :] == float(MAIN)
        scale = jnp.sum(jnp.where(ninth, wk[chunk, :], 0.0), axis=1, keepdims=True)
        pick = jnp.where(ninth, 1.0, 0.0).astype(BF16)
        x = dot(pick, tokens[...])
        g = dot(pick, grads[...]) * scale
        for c in range(nc):
            cols = slice(c * LANES, (c + 1) * LANES)
            ovs[:, c, :] = x[:, cols]
            ovs[:, nc + c, :] = g[:, cols]
        send[chunk, 2 * nc] = ovs[...].astype(BF16)
        pick = jnp.concatenate(hits, axis=0)
        scale = jnp.concatenate(scales, axis=0)
        pt[q] = pick.T.astype(BF16)
        pick = pick.astype(BF16)
        x = dot(pick, tokens[...])
        g = dot(pick, grads[...]) * scale
        for c in range(nc):
            cols = slice(c * LANES, (c + 1) * LANES)
            send[chunk, c] = x[:, cols].reshape(ns, MAIN, LANES).astype(BF16)
            send[chunk, nc + c] = g[:, cols].reshape(ns, MAIN, LANES).astype(BF16)

        @pl.when(q == 0)
        def _():
            pltpu.make_async_copy(send.at[0], ga.at[0], a_r.at[0]).start()

        def dispatch(k, carry):
            dev = {"expert": partner(k, True)}
            remote(send.at[k], ga.at[k], a_s.at[q], a_r.at[q], dev).start()
            return carry

        lax.fori_loop(jnp.maximum(base, 1), base + ns, dispatch, 0)
        return carry

    lax.fori_loop(0, nq, pack, 0)
    pot[...] = jnp.where(pk[...] == float(MAIN), 1.0, 0.0).T.astype(BF16)

    def at(q):
        return pl.ds(pl.multiple_of(q * rows, 16), rows)

    def stage1(q):
        mine = pl.ds(q * ns, ns)
        drain(ga.at[mine], a_r.at[q])
        remote(ga.at[mine], gp.at[mine], g_s.at[q], g_r.at[q], on_a).start()

    def stage2(q):
        base = q * ns
        drain(gp.at[pl.ds(base, ns)], g_r.at[q])
        main = pl.ds(pl.multiple_of(q * rows, 16), ns * MAIN)
        over = pl.ds(pl.multiple_of(q * rows + ns * MAIN, 16), ns)
        for j, buf in enumerate((ga, gp)):
            ovs[...] = buf[pl.ds(base, ns), 2 * nc].astype(F32)
            for c in range(nc):
                cols = slice(j * feat + c * LANES, j * feat + (c + 1) * LANES)
                xs[main, cols] = buf[pl.ds(base, ns), c].reshape(ns * MAIN, LANES)
                gs[main, cols] = buf[pl.ds(base, ns), nc + c].reshape(ns * MAIN, LANES)
                xs[over, cols] = ovs[:, c, :].astype(BF16)
                gs[over, cols] = ovs[:, nc + c, :].astype(BF16)
        x = xs[at(q), :]
        g = gs[at(q), :]
        ps[at(q), :gu] = dot(x, wt[1, :gu], LAST).astype(BF16)
        part = dot(g, wt[1, gu:], LAST)
        pad = jnp.zeros((rows, wide - gu - hid), F32)
        ps[at(q), gu:] = jnp.concatenate([part, pad], axis=1).astype(BF16)
        remote(ps.at[at(q)], pr.at[at(q)], p_s.at[q], p_r.at[q], on_b).start()
        gu_own[at(q), :] = dot(x, wt[0, :gu], LAST)
        h_own[at(q), :] = dot(g, wt[0, gu:], LAST)

    def stage3(q):
        drain(pr.at[at(q)], p_r.at[q])
        both = gu_own[at(q), :] + pr[at(q), :gu].astype(F32)
        hidden = h_own[at(q), :] + pr[at(q), gu : gu + hid].astype(F32)
        gate = both[:, :hid]
        up = both[:, hid:]
        sigma = jax.nn.sigmoid(gate)
        silu = gate * sigma
        gate_term = hidden * up * sigma * (1.0 + gate * (1.0 - sigma))
        up_term = hidden * silu
        tm[at(q), :gu] = jnp.concatenate([gate_term, up_term], axis=1).astype(BF16)
        pad = jnp.zeros((rows, wide - gu - hid), F32)
        tm[at(q), gu:] = jnp.concatenate([silu * up, pad], axis=1).astype(BF16)
        remote(tm.at[at(q)], tp.at[at(q)], t_s.at[q], t_r.at[q], on_b).start()

    def stage4(q):
        drain(tp.at[at(q)], t_r.at[q])
        mine = tm[at(q), :gu]
        theirs = tp[at(q), :gu]
        part = dot(mine, wt[0, :gu, feat:]) + dot(theirs, wt[1, :gu, feat:])
        ys[at(q), :] = part.astype(BF16)
        remote(ys.at[at(q)], yr.at[at(q)], y_s.at[q], y_r.at[q], on_a).start()
        y_own[at(q), :] = dot(mine, wt[0, :gu, :feat]) + dot(theirs, wt[1, :gu, :feat])

    def stage5(q):
        base = q * ns
        drain(yr.at[at(q)], y_r.at[q])
        slot = y_own[at(q), :] + yr[at(q), :].astype(F32)
        ovs[...] = jnp.zeros_like(ovs)
        for c in range(nc):
            cols = slice(c * LANES, (c + 1) * LANES)
            main = slot[: ns * MAIN, cols].reshape(ns, MAIN, LANES)
            back[pl.ds(base, ns), c] = main.astype(BF16)
            ovs[:, c, :] = slot[ns * MAIN :, cols]
        back[pl.ds(base, ns), nc] = ovs[...].astype(BF16)

        @pl.when(q == 0)
        def _():
            pltpu.make_async_copy(back.at[0], ret.at[0], b_r.at[0]).start()

        def answer(k, carry):
            dev = {"expert": partner(k, False)}
            remote(back.at[k], ret.at[k], b_s, b_r.at[q], dev).start()
            return carry

        lax.fori_loop(jnp.maximum(base, 1), base + ns, answer, 0)

    last = nq - 1
    middle = (last + 1) // 2
    ranges = [(0, middle), (middle, last)] if middle < last else [(0, last)]

    def weight_grads(block, first, stop):
        r = slice(first * rows, stop * rows)
        t = (tm, tp)[block]
        return dot(t[r, :gu], xs[r, :], FIRST), dot(t[r, gu : gu + hid], gs[r, :], FIRST)

    def step(t, carry):
        for lag, stage in enumerate((stage1, stage2, stage3, stage4, stage5)):
            q = t - lag
            if stage is stage2:

                @pl.when(q == 0)
                def _():
                    for load in loads:
                        load.wait()
                    for swap in swaps:
                        swap.wait_recv()

            @pl.when(jnp.logical_and(q >= 0, q < nq))
            def _():
                stage(q)

        for n, (first, stop) in enumerate(ranges):

            @pl.when(t - 3 == stop - 1)
            def _():
                for block in range(2):
                    both, down = weight_grads(block, first, stop)
                    if n == 0:
                        acc[block, :gu] = both
                        acc[block, gu:] = down
                    else:
                        acc[block, :gu] += both
                        acc[block, gu:] += down

        return carry

    lax.fori_loop(0, nq + 3, step, 0)

    outs = (o_gate, o_up, o_down)

    def piece(ref, n, h):
        return ref.at[pl.ds(n * hid, hid), pl.ds(h * feat, feat)]

    both, down = weight_grads(1, last, nq)
    dwp[:gu] = (acc[1, :gu] + both).astype(BF16)
    dwp[gu:] = (acc[1, gu:] + down).astype(BF16)
    theirs = [
        remote(
            piece(dwp, n, h), out.at[:, cols_of(x)], d_s.at[n, h], d_r.at[n, h], on_b
        )
        for n, out in enumerate(outs)
        for h, x in enumerate((xi, xa))
    ]
    for copy in theirs:
        copy.start()
    stage5(nq - 1)
    both, down = weight_grads(0, last, nq)
    dwo[:gu] = (acc[0, :gu] + both).astype(BF16)
    dwo[gu:] = (acc[0, gu:] + down).astype(BF16)
    mine = [
        pltpu.make_async_copy(piece(dwo, n, h), out.at[:, cols_of(x)], o_sem.at[n, h])
        for n, out in enumerate(outs)
        for h, x in enumerate((xi, xa))
    ]
    for copy in mine:
        copy.start()

    total = [jnp.zeros((tok, LANES), F32) for c in range(nc)]
    for q in range(nq):
        chunk = slice(q * ns, (q + 1) * ns)
        drain(ret.at[chunk], b_r.at[q])
        for c in range(nc):
            total[c] = total[c] + dot(pt[q], ret[chunk, c].reshape(ns * MAIN, LANES))
    ovf[...] = ret[:, nc].astype(F32)
    for c in range(nc):
        total[c] = total[c] + dot(pot[...], ovf[:, c, :].astype(BF16))
        o_tok[:, c * LANES : (c + 1) * LANES] = total[c].astype(BF16)

    for swap in swaps:
        swap.wait_send()
    drain(back.at[pl.ds(1, n_e - 1)], b_s)
    drain(send.at[pl.ds(0, ns - 1)], a_s.at[0])

    def flush_a(q, carry):
        drain(send.at[pl.ds(0, ns)], a_s.at[q])
        return carry

    lax.fori_loop(1, nq, flush_a, 0)

    def flush(q, carry):
        drain(ga.at[pl.ds(q * ns, ns)], g_s.at[q])
        drain(ps.at[at(q)], p_s.at[q])
        drain(tm.at[at(q)], t_s.at[q])
        drain(ys.at[at(q)], y_s.at[q])
        return carry

    lax.fori_loop(0, nq, flush, 0)
    for copy in mine:
        copy.wait()
    for copy in theirs:
        copy.wait_send()
        copy.wait_recv()


def body(tokens, out_grad, routes, combine, w_gate, w_up, w_down):
    n_e = lax.axis_size("expert")
    n_x = lax.axis_size("etp")
    tok, feat = tokens.shape
    hid, width = w_gate.shape[1:]
    nq = min(CHUNKS, n_e // 2)
    ns = n_e // nq
    slots = n_e * (MAIN + 1)
    nc = feat // LANES
    two = 2 * feat
    wide = (3 * hid + LANES - 1) // LANES * LANES
    vmem = pl.BlockSpec(memory_space=pltpu.VMEM)
    hbm = pl.BlockSpec(memory_space=pl.ANY)
    dma = pltpu.SemaphoreType.DMA
    grad_shape = jax.ShapeDtypeStruct((hid, width), BF16)
    outs = pl.pallas_call(
        functools.partial(kernel, n_e, n_x, nq),
        out_shape=(jax.ShapeDtypeStruct((tok, feat), BF16), grad_shape, grad_shape, grad_shape),
        in_specs=[pl.BlockSpec(memory_space=pltpu.HBM)] * 7,
        out_specs=(vmem, hbm, hbm, hbm),
        scratch_shapes=[
            pltpu.VMEM((tok, feat), BF16),
            pltpu.VMEM((tok, feat), BF16),
            pltpu.VMEM((routes.shape[1], tok), jnp.int32),
            pltpu.VMEM((routes.shape[1], tok), F32),
            pltpu.VMEM((2, 3 * hid, two), BF16),
            pltpu.VMEM((n_e, tok), F32),
            pltpu.VMEM((n_e, tok), F32),
            pltpu.VMEM((n_e, tok), F32),
            pltpu.VMEM((n_e, tok), F32),
            pltpu.VMEM((nq, tok, ns * MAIN), BF16),
            pltpu.VMEM((tok, n_e), BF16),
            pltpu.VMEM((n_e, MAIN, LANES), F32),
            pltpu.VMEM((n_e, 2 * nc + 1, MAIN, LANES), BF16),
            pltpu.VMEM((n_e, 2 * nc + 1, MAIN, LANES), BF16),
            pltpu.VMEM((n_e, 2 * nc + 1, MAIN, LANES), BF16),
            pltpu.VMEM((ns, MAIN, LANES), F32),
            pltpu.VMEM((slots, two), BF16),
            pltpu.VMEM((slots, two), BF16),
            pltpu.VMEM((slots, 2 * hid), F32),
            pltpu.VMEM((slots, hid), F32),
            pltpu.VMEM((slots, wide), BF16),
            pltpu.VMEM((slots, wide), BF16),
            pltpu.VMEM((slots, wide), BF16),
            pltpu.VMEM((slots, wide), BF16),
            pltpu.VMEM((slots, feat), F32),
            pltpu.VMEM((slots, feat), BF16),
            pltpu.VMEM((slots, feat), BF16),
            pltpu.VMEM((n_e, nc + 1, MAIN, LANES), BF16),
            pltpu.VMEM((n_e, nc + 1, MAIN, LANES), BF16),
            pltpu.VMEM((2, 3 * hid, two), F32),
            pltpu.VMEM((3 * hid, two), BF16),
            pltpu.VMEM((3 * hid, two), BF16),
            dma((4,)),
            dma((3, 2)),
            dma((3, 2)),
            dma((3, 2)),
        ]
        + [dma((nq,))] * 10
        + [dma(()), dma((nq,)), dma((3, 2)), dma((3, 2)), dma((3, 2))],
        compiler_params=pltpu.CompilerParams(
            collective_id=0, has_side_effects=True, vmem_limit_bytes=VMEM_MIB * 1024 * 1024
        ),
    )(
        *[
            pltpu.with_memory_space_constraint(a, pltpu.HBM)
            for a in (tokens, out_grad, routes.T, combine.T, w_gate[0], w_up[0], w_down[0])
        ]
    )
    grad_tokens, grad_gate, grad_up, grad_down = outs
    return grad_tokens, grad_gate[None], grad_up[None], grad_down[None]


def solution(mesh):
    placed = (
        P("expert", "etp"),
        P("expert", "etp"),
        P("expert", None),
        P("expert", None),
        P("expert", "etp", None),
        P("expert", "etp", None),
        P("expert", "etp", None),
    )
    return jax.shard_map(
        body,
        mesh=mesh,
        in_specs=placed,
        out_specs=(
            P("expert", "etp"),
            P("expert", "etp", None),
            P("expert", "etp", None),
            P("expert", "etp", None),
        ),
        check_vma=False,
    )
```

```python
import functools

import jax
import jax.numpy as jnp
from jax import lax
from jax.experimental import pallas as pl
from jax.experimental.pallas import tpu as pltpu
from jax.sharding import PartitionSpec as P

MESH = pl.DeviceIdType.MESH
BF16 = jnp.bfloat16
F32 = jnp.float32
LANES = 128
MAIN = 8
HALF = 4
STRIDE = 3
SPAN = 8
CHUNKS = 8
VMEM_MIB = 48


def dot(a, b, dims=(((1,), (0,)), ((), ()))):
    return lax.dot_general(a, b, dims, preferred_element_type=F32)


LAST = (((1,), (1,)), ((), ()))
FIRST = (((0,), (0,)), ((), ()))


def kernel(
    n_e, n_x, nq,
    tok_h, grad_h, route_h, comb_h, wg_h, wu_h, wd_h,
    o_tok, o_gate, o_up, o_down,
    tokens, grads, routes, combine, wt, place_t, weight_t, pk, wk, pt, pot, ovf, send, ga, gp, ovs, xs, gs,
    gu_own, h_own, ps, pr, tm, tp, y_own, ys, yr, back, ret, acc, dwo, dwp,
    in_sem, wl_sem, w_s, w_r, a_s, a_r, g_s, g_r, p_s, p_r, t_s, t_r, y_s, y_r, b_s, b_r, d_s, d_r, o_sem,
):
    tok, feat = tokens.shape
    top = routes.shape[0]
    nc = feat // LANES
    hid = wg_h.shape[0]
    gu = 2 * hid
    wide = ps.shape[1]
    ns = n_e // nq
    rows = ns * (MAIN + 1)
    me = lax.axis_index("expert")
    xi = lax.axis_index("etp")
    parity = lax.rem(me, 2)
    turn = lax.rem(xi + parity, n_x)
    xa = lax.rem(turn + 1 - 2 * lax.rem(turn, 2) + n_x - parity, n_x)
    xb = lax.rem(n_x - 1 - turn + n_x - parity, n_x)
    xd = lax.rem(n_x - 1 - turn + 1 - 2 * lax.rem(n_x - 1 - turn, 2) + n_x - parity, n_x)
    on_a, on_b = {"etp": xa}, {"etp": xb}

    def remote(src, dst, s, r, dev):
        return pltpu.make_async_remote_copy(
            src_ref=src, dst_ref=dst, send_sem=s, recv_sem=r, device_id=dev, device_id_type=MESH
        )

    def drain(ref, sem):
        pltpu.make_async_copy(ref, ref, sem).wait()

    def cols_of(x):
        return pl.ds(pl.multiple_of(x * feat, LANES), feat)

    span = min(SPAN, n_e // 2)
    layers = n_e // (2 * span)

    def partner(k, ahead):
        lo, hi = lax.rem(k, span), lax.rem(k // span, layers)
        step_c = k // (span * layers)
        step_y = lax.rem(lo * STRIDE, span)
        step_z = lax.rem(step_y + hi, layers)
        if not ahead:
            step_c, step_y, step_z = 2 - step_c, span - step_y, layers - step_z
        z = lax.rem(me // (2 * span) + step_z, layers)
        y = lax.rem(lax.rem(me // 2, span) + step_y, span)
        return (z * span + y) * 2 + lax.rem(lax.rem(me, 2) + step_c, 2)

    reads = [
        pltpu.make_async_copy(src, dst, in_sem.at[n])
        for n, (src, dst) in enumerate(
            ((route_h, routes), (comb_h, combine), (tok_h, tokens), (grad_h, grads))
        )
    ]
    for read in reads:
        read.start()

    bar = pltpu.get_barrier_semaphore()
    for dev in (on_a, on_b):
        pl.semaphore_signal(bar, inc=1, device_id=dev, device_id_type=MESH)

    def greet(off, carry):
        pl.semaphore_signal(
            bar, inc=1, device_id={"expert": lax.rem(me + off, n_e)}, device_id_type=MESH
        )
        return carry

    lax.fori_loop(1, n_e, greet, 0)

    weights = (wg_h, wu_h, wd_h)
    loads = [
        pltpu.make_async_copy(
            src.at[:, cols_of(x)],
            wt.at[0, pl.ds(n * hid, hid), pl.ds(h * feat, feat)],
            wl_sem.at[n, h],
        )
        for n, src in enumerate(weights)
        for h, x in enumerate((xi, xa))
    ]
    for load in loads:
        load.start()

    for read in reads:
        read.wait()
    label = lax.broadcasted_iota(jnp.int32, (n_e, tok), 0)
    hit = jnp.zeros((n_e, tok), F32)
    weight = jnp.zeros((n_e, tok), F32)
    for k in range(top):
        same = routes[k : k + 1, :] == label
        hit = hit + jnp.where(same, 1.0, 0.0)
        weight = weight + jnp.where(same, combine[k : k + 1, :], 0.0)
    earlier = (
        lax.broadcasted_iota(jnp.int32, (tok, tok), 0)
        < lax.broadcasted_iota(jnp.int32, (tok, tok), 1)
    )
    earlier = jnp.where(earlier, 1.0, 0.0).astype(BF16)
    place_t[...] = jnp.where(hit > 0.5, dot(hit.astype(BF16), earlier), -1.0)
    weight_t[...] = weight

    pl.semaphore_wait(bar, n_e - 1 + 2)

    swaps = [
        remote(
            src.at[:, cols_of(x)],
            wt.at[1, pl.ds(n * hid, hid), pl.ds(h * feat, feat)],
            w_s.at[n, h], w_r.at[n, h], on_b,
        )
        for n, src in enumerate(weights)
        for h, x in enumerate((xb, xd))
    ]
    for swap in swaps:
        swap.start()

    slot_id = lax.broadcasted_iota(jnp.int32, (MAIN, tok), 0).astype(F32)

    def pack(q, carry):
        base = q * ns
        hits, scales = [], []
        for u in range(ns):
            e = partner(base + u, True)
            pk[pl.ds(base + u, 1), :] = place_t[pl.ds(e, 1), :]
            wk[pl.ds(base + u, 1), :] = weight_t[pl.ds(e, 1), :]
            row = jnp.broadcast_to(place_t[pl.ds(e, 1), :], (MAIN, tok))
            wrow = jnp.broadcast_to(weight_t[pl.ds(e, 1), :], (MAIN, tok))
            same = row == slot_id
            hits.append(jnp.where(same, 1.0, 0.0))
            scales.append(jnp.sum(jnp.where(same, wrow, 0.0), axis=1, keepdims=True))
        chunk = pl.ds(base, ns)
        ninth = pk[chunk, :] == float(MAIN)
        scale = jnp.sum(jnp.where(ninth, wk[chunk, :], 0.0), axis=1, keepdims=True)
        pick = jnp.where(ninth, 1.0, 0.0).astype(BF16)
        x = dot(pick, tokens[...])
        g = dot(pick, grads[...]) * scale
        for c in range(nc):
            cols = slice(c * LANES, (c + 1) * LANES)
            ovs[:, c, :] = x[:, cols]
            ovs[:, nc + c, :] = g[:, cols]
        send[chunk, 2 * nc] = ovs[...].astype(BF16)
        pick = jnp.concatenate(hits, axis=0)
        scale = jnp.concatenate(scales, axis=0)
        pt[q] = pick.T.astype(BF16)
        pick = pick.astype(BF16)
        x = dot(pick, tokens[...])
        g = dot(pick, grads[...]) * scale
        for c in range(nc):
            cols = slice(c * LANES, (c + 1) * LANES)
            send[chunk, c] = x[:, cols].reshape(ns, MAIN, LANES).astype(BF16)
            send[chunk, nc + c] = g[:, cols].reshape(ns, MAIN, LANES).astype(BF16)

        @pl.when(q == 0)
        def _():
            pltpu.make_async_copy(send.at[0], ga.at[0], a_r.at[0]).start()

        def dispatch(k, carry):
            dev = {"expert": partner(k, True)}
            remote(send.at[k], ga.at[k], a_s.at[q], a_r.at[q], dev).start()
            return carry

        lax.fori_loop(jnp.maximum(base, 1), base + ns, dispatch, 0)
        return carry

    lax.fori_loop(0, nq, pack, 0)
    pot[...] = jnp.where(pk[...] == float(MAIN), 1.0, 0.0).T.astype(BF16)

    def at(q):
        return pl.ds(pl.multiple_of(q * rows, 16), rows)

    def stage1(q):
        mine = pl.ds(q * ns, ns)
        drain(ga.at[mine], a_r.at[q])
        remote(ga.at[mine], gp.at[mine], g_s.at[q], g_r.at[q], on_a).start()

    def stage2(q):
        base = q * ns
        drain(gp.at[pl.ds(base, ns)], g_r.at[q])
        main = pl.ds(pl.multiple_of(q * rows, 16), ns * MAIN)
        over = pl.ds(pl.multiple_of(q * rows + ns * MAIN, 16), ns)
        for j, buf in enumerate((ga, gp)):
            ovs[...] = buf[pl.ds(base, ns), 2 * nc].astype(F32)
            for c in range(nc):
                cols = slice(j * feat + c * LANES, j * feat + (c + 1) * LANES)
                xs[main, cols] = buf[pl.ds(base, ns), c].reshape(ns * MAIN, LANES)
                gs[main, cols] = buf[pl.ds(base, ns), nc + c].reshape(ns * MAIN, LANES)
                xs[over, cols] = ovs[:, c, :].astype(BF16)
                gs[over, cols] = ovs[:, nc + c, :].astype(BF16)
        x = xs[at(q), :]
        g = gs[at(q), :]
        ps[at(q), :gu] = dot(x, wt[1, :gu], LAST).astype(BF16)
        part = dot(g, wt[1, gu:], LAST)
        pad = jnp.zeros((rows, wide - gu - hid), F32)
        ps[at(q), gu:] = jnp.concatenate([part, pad], axis=1).astype(BF16)
        remote(ps.at[at(q)], pr.at[at(q)], p_s.at[q], p_r.at[q], on_b).start()
        gu_own[at(q), :] = dot(x, wt[0, :gu], LAST)
        h_own[at(q), :] = dot(g, wt[0, gu:], LAST)

    def stage3(q):
        drain(pr.at[at(q)], p_r.at[q])
        both = gu_own[at(q), :] + pr[at(q), :gu].astype(F32)
        hidden = h_own[at(q), :] + pr[at(q), gu : gu + hid].astype(F32)
        gate = both[:, :hid]
        up = both[:, hid:]
        sigma = jax.nn.sigmoid(gate)
        silu = gate * sigma
        gate_term = hidden * up * sigma * (1.0 + gate * (1.0 - sigma))
        up_term = hidden * silu
        tm[at(q), :gu] = jnp.concatenate([gate_term, up_term], axis=1).astype(BF16)
        pad = jnp.zeros((rows, wide - gu - hid), F32)
        tm[at(q), gu:] = jnp.concatenate([silu * up, pad], axis=1).astype(BF16)
        remote(tm.at[at(q)], tp.at[at(q)], t_s.at[q], t_r.at[q], on_b).start()

    def stage4(q):
        drain(tp.at[at(q)], t_r.at[q])
        mine = tm[at(q), :gu]
        theirs = tp[at(q), :gu]
        part = dot(mine, wt[0, :gu, feat:]) + dot(theirs, wt[1, :gu, feat:])
        ys[at(q), :] = part.astype(BF16)
        remote(ys.at[at(q)], yr.at[at(q)], y_s.at[q], y_r.at[q], on_a).start()

    def stage4_own(q):
        mine = tm[at(q), :gu]
        theirs = tp[at(q), :gu]
        y_own[at(q), :] = dot(mine, wt[0, :gu, :feat]) + dot(theirs, wt[1, :gu, :feat])

    def stage5(q):
        base = q * ns
        drain(yr.at[at(q)], y_r.at[q])
        slot = y_own[at(q), :] + yr[at(q), :].astype(F32)
        for c in range(nc):
            cols = slice(c * LANES, (c + 1) * LANES)
            main = slot[: ns * MAIN, cols].reshape(ns, MAIN, LANES)
            for h in range(2):
                half = main[:, h * HALF : (h + 1) * HALF]
                back[pl.ds(base, ns), 2 * c + h] = half.astype(BF16)
            ovs[:, c, :] = slot[ns * MAIN :, cols]
        back[pl.ds(base, ns), 2 * nc] = ovs[:, :HALF].astype(BF16)

        @pl.when(q == 0)
        def _():
            pltpu.make_async_copy(back.at[0], ret.at[0], b_r.at[0]).start()

        def answer(k, carry):
            dev = {"expert": partner(k, False)}
            remote(back.at[k], ret.at[k], b_s, b_r.at[q], dev).start()
            return carry

        lax.fori_loop(jnp.maximum(base, 1), base + ns, answer, 0)

    last = nq - 1
    middle = (last + 1) // 2
    ranges = [(0, middle), (middle, last)] if middle < last else [(0, last)]

    def weight_grads(block, first, stop):
        r = slice(first * rows, stop * rows)
        t = (tm, tp)[block]
        return dot(t[r, :gu], xs[r, :], FIRST), dot(t[r, gu : gu + hid], gs[r, :], FIRST)

    def step(t, carry):
        for lag, stage in enumerate((stage1, stage2, stage3, stage4, stage5)):
            q = t - lag
            if stage is stage2:

                @pl.when(q == 0)
                def _():
                    for load in loads:
                        load.wait()
                    for swap in swaps:
                        swap.wait_recv()

            @pl.when(jnp.logical_and(q >= 0, q < nq))
            def _():
                stage(q)
                if stage is stage4:
                    stage4_own(q)

        for n, (first, stop) in enumerate(ranges):

            @pl.when(t - 3 == stop - 1)
            def _():
                for block in (0, 1) if n == 0 else (1,):
                    both, down = weight_grads(block, first, stop)
                    if n == 0:
                        acc[block, :gu] = both
                        acc[block, gu:] = down
                    else:
                        acc[block, :gu] += both
                        acc[block, gu:] += down

        return carry

    lax.fori_loop(0, nq + 2, step, 0)
    stage4(nq - 1)

    outs = (o_gate, o_up, o_down)

    def piece(ref, n, h):
        return ref.at[pl.ds(n * hid, hid), pl.ds(h * feat, feat)]

    both, down = weight_grads(1, last, nq)
    dwp[:gu] = (acc[1, :gu] + both).astype(BF16)
    dwp[gu:] = (acc[1, gu:] + down).astype(BF16)
    theirs = [
        remote(
            piece(dwp, n, h), out.at[:, cols_of(x)], d_s.at[n, h], d_r.at[n, h], on_b
        )
        for n, out in enumerate(outs)
        for h, x in enumerate((xi, xa))
    ]
    for copy in theirs:
        copy.start()
    stage4_own(nq - 1)
    stage5(nq - 2)
    stage5(nq - 1)
    both, down = weight_grads(0, ranges[0][1], nq)
    dwo[:gu] = (acc[0, :gu] + both).astype(BF16)
    dwo[gu:] = (acc[0, gu:] + down).astype(BF16)
    mine = [
        pltpu.make_async_copy(piece(dwo, n, h), out.at[:, cols_of(x)], o_sem.at[n, h])
        for n, out in enumerate(outs)
        for h, x in enumerate((xi, xa))
    ]
    for copy in mine:
        copy.start()

    total = [jnp.zeros((tok, LANES), F32) for c in range(nc)]
    for q in range(nq):
        chunk = slice(q * ns, (q + 1) * ns)
        drain(ret.at[chunk], b_r.at[q])
        for c in range(nc):
            for h in range(2):
                ovs[:, h * HALF : (h + 1) * HALF] = ret[chunk, 2 * c + h].astype(F32)
            part = ovs[...].reshape(ns * MAIN, LANES).astype(BF16)
            total[c] = total[c] + dot(pt[q], part)
    ovf[:, :HALF] = ret[:, 2 * nc].astype(F32)
    for c in range(nc):
        total[c] = total[c] + dot(pot[...], ovf[:, c, :].astype(BF16))
        o_tok[:, c * LANES : (c + 1) * LANES] = total[c].astype(BF16)

    for swap in swaps:
        swap.wait_send()
    drain(back.at[pl.ds(1, n_e - 1)], b_s)
    drain(send.at[pl.ds(0, ns - 1)], a_s.at[0])

    def flush_a(q, carry):
        drain(send.at[pl.ds(0, ns)], a_s.at[q])
        return carry

    lax.fori_loop(1, nq, flush_a, 0)

    def flush(q, carry):
        drain(ga.at[pl.ds(q * ns, ns)], g_s.at[q])
        drain(ps.at[at(q)], p_s.at[q])
        drain(tm.at[at(q)], t_s.at[q])
        drain(ys.at[at(q)], y_s.at[q])
        return carry

    lax.fori_loop(0, nq, flush, 0)
    for copy in mine:
        copy.wait()
    for copy in theirs:
        copy.wait_send()
        copy.wait_recv()


def body(tokens, out_grad, routes, combine, w_gate, w_up, w_down):
    n_e = lax.axis_size("expert")
    n_x = lax.axis_size("etp")
    tok, feat = tokens.shape
    hid, width = w_gate.shape[1:]
    nq = min(CHUNKS, n_e // 2)
    ns = n_e // nq
    slots = n_e * (MAIN + 1)
    nc = feat // LANES
    two = 2 * feat
    wide = (3 * hid + LANES - 1) // LANES * LANES
    vmem = pl.BlockSpec(memory_space=pltpu.VMEM)
    hbm = pl.BlockSpec(memory_space=pl.ANY)
    dma = pltpu.SemaphoreType.DMA
    grad_shape = jax.ShapeDtypeStruct((hid, width), BF16)
    outs = pl.pallas_call(
        functools.partial(kernel, n_e, n_x, nq),
        out_shape=(jax.ShapeDtypeStruct((tok, feat), BF16), grad_shape, grad_shape, grad_shape),
        in_specs=[pl.BlockSpec(memory_space=pltpu.HBM)] * 7,
        out_specs=(vmem, hbm, hbm, hbm),
        scratch_shapes=[
            pltpu.VMEM((tok, feat), BF16),
            pltpu.VMEM((tok, feat), BF16),
            pltpu.VMEM((routes.shape[1], tok), jnp.int32),
            pltpu.VMEM((routes.shape[1], tok), F32),
            pltpu.VMEM((2, 3 * hid, two), BF16),
            pltpu.VMEM((n_e, tok), F32),
            pltpu.VMEM((n_e, tok), F32),
            pltpu.VMEM((n_e, tok), F32),
            pltpu.VMEM((n_e, tok), F32),
            pltpu.VMEM((nq, tok, ns * MAIN), BF16),
            pltpu.VMEM((tok, n_e), BF16),
            pltpu.VMEM((n_e, MAIN, LANES), F32),
            pltpu.VMEM((n_e, 2 * nc + 1, MAIN, LANES), BF16),
            pltpu.VMEM((n_e, 2 * nc + 1, MAIN, LANES), BF16),
            pltpu.VMEM((n_e, 2 * nc + 1, MAIN, LANES), BF16),
            pltpu.VMEM((ns, MAIN, LANES), F32),
            pltpu.VMEM((slots, two), BF16),
            pltpu.VMEM((slots, two), BF16),
            pltpu.VMEM((slots, 2 * hid), F32),
            pltpu.VMEM((slots, hid), F32),
            pltpu.VMEM((slots, wide), BF16),
            pltpu.VMEM((slots, wide), BF16),
            pltpu.VMEM((slots, wide), BF16),
            pltpu.VMEM((slots, wide), BF16),
            pltpu.VMEM((slots, feat), F32),
            pltpu.VMEM((slots, feat), BF16),
            pltpu.VMEM((slots, feat), BF16),
            pltpu.VMEM((n_e, 2 * nc + 1, HALF, LANES), BF16),
            pltpu.VMEM((n_e, 2 * nc + 1, HALF, LANES), BF16),
            pltpu.VMEM((2, 3 * hid, two), F32),
            pltpu.VMEM((3 * hid, two), BF16),
            pltpu.VMEM((3 * hid, two), BF16),
            dma((4,)),
            dma((3, 2)),
            dma((3, 2)),
            dma((3, 2)),
        ]
        + [dma((nq,))] * 10
        + [dma(()), dma((nq,)), dma((3, 2)), dma((3, 2)), dma((3, 2))],
        compiler_params=pltpu.CompilerParams(
            collective_id=0, has_side_effects=True, vmem_limit_bytes=VMEM_MIB * 1024 * 1024
        ),
    )(
        *[
            pltpu.with_memory_space_constraint(a, pltpu.HBM)
            for a in (tokens, out_grad, routes.T, combine.T, w_gate[0], w_up[0], w_down[0])
        ]
    )
    grad_tokens, grad_gate, grad_up, grad_down = outs
    return grad_tokens, grad_gate[None], grad_up[None], grad_down[None]


def solution(mesh):
    placed = (
        P("expert", "etp"),
        P("expert", "etp"),
        P("expert", None),
        P("expert", None),
        P("expert", "etp", None),
        P("expert", "etp", None),
        P("expert", "etp", None),
    )
    return jax.shard_map(
        body,
        mesh=mesh,
        in_specs=placed,
        out_specs=(
            P("expert", "etp"),
            P("expert", "etp", None),
            P("expert", "etp", None),
            P("expert", "etp", None),
        ),
        check_vma=False,
    )
```
